32 devices in a mesh: group: 2 (over x), row: 16 (over z, y, core).
Axes of the slice: x: 2, y: 2, z: 4, core: 2. Of those that a mesh axis runs over, the one named last changes fastest.
Arguments:
- pair_rep: float32 [256, 128, 128], P(('group', 'row')), parts along dimension 0, may hold values from -7 to 7
- token_mask: int32 [256], P('group'), parts along dimension 0, may hold values 0 or 1
- ln_gain: float32 [2, 128], replicated, may hold values from 0.5 to 1.5
- w_proj: bfloat16 [2, 128, 512], replicated, may hold values from -0.5 to 0.5
- w_tri: bfloat16 [2, 128, 4], replicated, may hold values from -3 to 3
- gate_bias: float32 [2, 128], replicated, may hold values from -6 to 6
- w_out: bfloat16 [2, 128, 128], replicated, may hold values from -0.5 to 0.5
- out_bias: float32 [2, 128], replicated, may hold values from -3 to 3
Outputs:
- pair_next: float32 [256, 128, 128], P('group', 'row'), parts along dimension 0
The draws below stay inside these ranges and needn't reach their ends.
There are 2 independent parts, one for each index of `group`. The reference program is written for one: setup_inputs(seed, part) draws one part's arguments, and reference() takes and returns one part's arrays. A program takes and returns all parts, laid end to end along the dimension named above; an argument that names none is the same for every part. Nothing has to cross between parts.
All inputs are finite; a program needn't handle non-finite values.
Results may differ from the reference program's by a relative error of at most 0.009.
Values may be sent and summed in bfloat16 or wider, within the bound.
No kernel may reach another device: no remote copies, remote signals or barrier semaphores. Data moves between devices by JAX's collectives and lax.ppermute only.
A program may use at most 128 MiB of HBM per device.

```python
import jax
import jax.numpy as jnp
from jax import lax

C = 128
H = 4
DH = 32
L = 128


def draw_pair_rep(key, part):
    return jnp.clip(jax.random.normal(key, (L, L, C), jnp.float32), -4.0, 4.0)


def draw_w_tri(key, part):
    jitter = jnp.clip(jax.random.normal(key, (2, C, H), jnp.float32), -4.0, 4.0) * C ** (-0.5)
    return jitter.astype(jnp.bfloat16)


def touch_ends(result, own_key, least, largest):
    dims = result.shape
    place = [jax.random.randint(jax.random.fold_in(own_key, axis), (), 0, dims[axis]) for axis in range(len(dims))]
    result = result.at[tuple(place)].set(least)
    longest = dims.index(max(dims))
    place[longest] = (place[longest] + 1) % dims[longest]
    return result.at[tuple(place)].set(largest)


def normal_values(key, shape, scale, bound, held_as=jnp.bfloat16):
    array = jax.random.normal(key, shape, jnp.float32) * scale
    return jnp.minimum(jnp.maximum(array, -bound), bound).astype(held_as)


def setup_inputs(seed: int = 0, part: int = 0) -> dict:
    key_of = jax.random.split(jax.random.key(seed), 9)
    part_keys = jax.random.split(jax.random.fold_in(key_of[8], part), 9)
    pair_rep = draw_pair_rep(jax.random.fold_in(jax.random.fold_in(key_of[8], part), 71), part)
    token_mask = touch_ends((jax.random.randint(part_keys[1], (L,), 0, 8) < 7).astype(jnp.int32), jax.random.fold_in(part_keys[1], 1), 0, 1)
    ln_gain = jnp.clip(1.0 + 0.1 * jax.random.normal(key_of[2], (2, C), jnp.float32), 0.5, 1.5)
    w_proj = normal_values(key_of[3], (2, C, 4 * H * DH), C ** -0.5, 0.5)
    w_tri = draw_w_tri(jax.random.fold_in(key_of[8], 71), part)
    gate_bias = normal_values(key_of[5], (2, H * DH), 2.0, 6.0, jnp.float32)
    w_out = normal_values(key_of[6], (2, H * DH, C), (H * DH) ** -0.5, 0.5)
    out_bias = normal_values(key_of[7], (2, C), 0.5, 3.0, jnp.float32)
    return {"pair_rep": pair_rep, "token_mask": token_mask, "ln_gain": ln_gain, "w_proj": w_proj, "w_tri": w_tri, "gate_bias": gate_bias, "w_out": w_out, "out_bias": out_bias}


def normed(pair_rep, gain):
    centre = lax.optimization_barrier(jnp.mean(pair_rep, axis=-1, keepdims=True))
    shifted = pair_rep - centre
    spread = lax.optimization_barrier(jnp.mean(shifted * shifted, axis=-1, keepdims=True))
    return (shifted * lax.rsqrt(spread + 1e-05) * gain).astype(jnp.bfloat16)

def attend(queries, key_rows, values, tri_bias, keep_mask, head_count):
    query_len = queries.shape[0]
    key_count = key_rows.shape[0]
    head_dim = queries.shape[1] // head_count
    scores = jnp.einsum('jhd,khd->hjk', queries.reshape(query_len, head_count, head_dim).astype(jnp.float32), key_rows.reshape(key_count, head_count, head_dim).astype(jnp.float32))
    scores = scores + tri_bias.astype(jnp.float32)
    scores = jnp.where(keep_mask[None, None, :], scores, jnp.float32(-1000000000.0))
    row_max = lax.optimization_barrier(jnp.max(scores, axis=2, keepdims=True))
    weights = jnp.exp(scores - row_max)
    probabilities = (weights / lax.optimization_barrier(jnp.sum(weights, axis=2, keepdims=True))).astype(jnp.bfloat16)
    mixture = jnp.einsum('hjk,khd->jhd', probabilities.astype(jnp.float32), values.reshape(key_count, head_count, head_dim).astype(jnp.float32))
    return mixture.reshape(query_len, head_count * head_dim)

def one_pass(pair_rep, token_mask, gain, w_proj, w_tri, gate_bias, w_out, out_bias):
    normal_x = normed(pair_rep, gain)
    tri_bias = jnp.einsum('jkc,ch->hjk', normal_x.astype(jnp.float32), w_tri.astype(jnp.float32)).astype(jnp.bfloat16)
    head_count = w_tri.shape[1]
    inner_width = w_proj.shape[1] // 4
    scaling = DH ** (-0.5)

    def one_row(row_items):
        x_row, flag = row_items
        projected = jnp.dot(x_row, w_proj, preferred_element_type=jnp.float32)
        queries = (projected[:, :inner_width] * scaling).astype(jnp.bfloat16)
        key_rows = projected[:, inner_width:2 * inner_width].astype(jnp.bfloat16)
        values = projected[:, 2 * inner_width:3 * inner_width].astype(jnp.bfloat16)
        gate_act = jax.nn.sigmoid(projected[:, 3 * inner_width:] + gate_bias)
        keep_mask = flag * token_mask > 0
        mixture = attend(queries, key_rows, values, tri_bias, keep_mask, head_count)
        joined = (gate_act * mixture).astype(jnp.bfloat16)
        return jnp.dot(joined, w_out, preferred_element_type=jnp.float32) + out_bias
    return lax.map(one_row, (normal_x, token_mask))

def reference(pair_rep, token_mask, ln_gain, w_proj, w_tri, gate_bias, w_out, out_bias):
    stacked = pair_rep + one_pass(pair_rep, token_mask, ln_gain[0], w_proj[0], w_tri[0], gate_bias[0], w_out[0], out_bias[0])
    turned = jnp.swapaxes(stacked, 0, 1)
    second = one_pass(turned, token_mask, ln_gain[1], w_proj[1], w_tri[1], gate_bias[1], w_out[1], out_bias[1])
    return stacked + jnp.swapaxes(second, 0, 1)
```

```python
import functools

import jax
import jax.numpy as jnp
from jax import lax
from jax.experimental import pallas as pl
from jax.experimental.pallas import tpu as pltpu
from jax.sharding import PartitionSpec as P

LANES = 128
VMEM_BYTES = 24 * 2**20
EARLY_BYTES = 4 * 2**20
F32 = jnp.float32
BF16 = jnp.bfloat16
MASKED = -1000000000.0
LOG2E = 1.4426950408889634


def dot(a, b, dims=((1,), (0,))):
    return lax.dot_general(a, b, (dims, ((), ())), preferred_element_type=F32)


def interleave(streams, lag):
    waiting = [(i * lag, stream) for i, stream in enumerate(streams)]
    turn = 0
    while waiting:
        left = []
        for start, stream in waiting:
            if start <= turn and next(stream, waiting) is waiting:
                continue
            left.append((start, stream))
        waiting = left
        turn += 1


def normed(x, gain):
    centre = jnp.mean(x, axis=-1, keepdims=True)
    shifted = x - centre
    spread = jnp.mean(shifted * shifted, axis=-1, keepdims=True)
    return (shifted * lax.rsqrt(spread + 1e-05) * gain).astype(BF16)


def head_masks(heads, width):
    dim = width // heads
    down = lax.broadcasted_iota(jnp.int32, (width, LANES), 0) // dim
    across = lax.broadcasted_iota(jnp.int32, (LANES, width), 1) // dim
    return (
        [(down == h).astype(F32).astype(BF16) for h in range(heads)],
        [(across == h).astype(F32).astype(BF16) for h in range(heads)],
    )


def key_block(kt, picked, down):
    spread = []
    for h in picked:
        for t in range(kt.shape[1] // LANES):
            spread.append(kt[:, t * LANES : (t + 1) * LANES] * down[h])
    return jnp.concatenate(spread, axis=1)


def value_block(v, picked, across):
    parts = []
    for h in picked:
        for t in range(v.shape[0] // LANES):
            piece = v[t * LANES : (t + 1) * LANES] * across[h]
            parts.append(jnp.concatenate([piece, across[h]], axis=1))
    return jnp.concatenate(parts, axis=0)


def softened(scores, kept):
    part = jnp.where(kept, scores, F32(MASKED))
    return jnp.exp2(part - jnp.max(part, axis=1, keepdims=True)).astype(BF16)


def pairs_of(heads):
    return [tuple(range(h, min(h + 2, heads))) for h in range(0, heads, 2)]


def bias_kernel(x_ref, gain_ref, w_tri_ref, send_ref, norm_ref, rows_ref, held_ref, sems):
    rows, length, _ = x_ref.shape
    heads = w_tri_ref.shape[1]
    copies = [pltpu.make_async_copy(x_ref.at[i], held_ref.at[i], sems.at[i]) for i in range(rows)]
    for copy in copies:
        copy.start()

    def stream(i, t):
        span = slice(t * LANES, (t + 1) * LANES)
        if t == 0:
            copies[i].wait()
        x = held_ref[i, span, :]
        shifted = x - jnp.mean(x, axis=-1, keepdims=True)
        yield
        spread = jnp.mean(shifted * shifted, axis=-1, keepdims=True)
        yield
        x = (shifted * lax.rsqrt(spread + 1e-05) * gain_ref[0:1, :]).astype(BF16)
        norm_ref[i, span, :] = x
        yield
        rows_ref[pl.ds(t * heads * rows + i, heads, stride=rows), :] = dot(w_tri_ref[0], x, ((1,), (1,)))

    interleave([stream(i, t) for i in range(rows) for t in range(length // LANES)], 1)
    packed = rows_ref[...].astype(BF16)
    for d in range(send_ref.shape[0]):
        send_ref[d] = packed


def project_kernel(heads, early, norm_ref, flag_ref, mask_ref, w_ref, gate_bias_ref, *out_refs):
    q_ref, k_ref, v_ref, g_ref, keep_ref = out_refs[:5]
    rows, length, width = q_ref.shape
    scaling = (width // heads) ** (-0.5)
    down, _ = head_masks(heads, width)
    w = w_ref[0]
    w_keys = w[:, width : 2 * width].T
    first = lax.axis_index("row") * rows

    def stream(i):
        x = norm_ref[i]
        q = (dot(x, w[:, :width]) * scaling).astype(BF16)
        q_ref[i] = q
        kt = dot(w_keys, x, ((1,), (1,))).astype(BF16)
        k_ref[i] = kt
        yield
        v_ref[i] = dot(x, w[:, 2 * width : 3 * width]).astype(BF16)
        g_ref[i] = jax.nn.sigmoid(dot(x, w[:, 3 * width :]) + gate_bias_ref[0:1, :])
        keep_ref[i : i + 1, :] = mask_ref[...] * flag_ref[first + i]
        yield
        if early:
            for picked in pairs_of(heads):
                at = slice(picked[0] * length, (picked[-1] + 1) * length)
                out_refs[5][i, :, at] = dot(q, key_block(kt, picked, down)) * LOG2E
                yield

    interleave([stream(i) for i in range(rows)], 2)


def first_kernel(
    early, x_ref, q_ref, k_ref, v_ref, g_ref, got_ref, keep_ref, gain_ref, w_tri_ref, w_out_ref, out_bias_ref,
    *more_refs,
):
    send_ref, bias_ref, rows_ref = more_refs[-3:]
    rows, length, width = q_ref.shape
    heads = w_tri_ref.shape[1]
    parties = send_ref.shape[0]
    share = length // parties
    blocks = length // LANES
    for h in range(heads):
        for t in range(blocks):
            at = (t * heads + h) * rows
            bias_ref[:, h * length + t * LANES : h * length + (t + 1) * LANES] = (
                got_ref[:, at : at + rows, :].astype(F32).reshape(length, LANES) * LOG2E
            )
    down, across = head_masks(heads, width)

    def stream(i, t):
        span = slice(t * LANES, (t + 1) * LANES)
        kept = jnp.broadcast_to(keep_ref[i : i + 1, :], (LANES, length)) > 0
        both = None
        for picked in pairs_of(heads):
            weights = []
            scores = None
            if not early:
                scores = dot(q_ref[i, span, :], key_block(k_ref[i], picked, down)) * LOG2E
            for n, h in enumerate(picked):
                at = slice(h * length, (h + 1) * length)
                part = more_refs[0][i, span, at] if early else scores[:, n * length : (n + 1) * length]
                weights.append(softened(part + bias_ref[span, at], kept))
                yield
            term = dot(jnp.concatenate(weights, axis=1), value_block(v_ref[i], picked, across))
            both = term if both is None else both + term
            yield
        joined = (g_ref[i, span, :] * (both[:, :width] / both[:, width:])).astype(BF16)
        stacked = x_ref[i, span, :] + (dot(joined, w_out_ref[0]) + out_bias_ref[0:1, :])
        reach = LANES // share
        send_ref[t * reach : (t + 1) * reach, i * share : (i + 1) * share, :] = stacked.reshape(
            reach, share, stacked.shape[1]
        ).astype(BF16)
        yield
        shifted = stacked - jnp.mean(stacked, axis=-1, keepdims=True)
        yield
        spread = jnp.mean(shifted * shifted, axis=-1, keepdims=True)
        yield
        x = (shifted * lax.rsqrt(spread + 1e-05) * gain_ref[1:2, :]).astype(BF16)
        rows_ref[pl.ds(t * heads * rows + i, heads, stride=rows), :] = dot(w_tri_ref[0], x, ((1,), (1,)))

    interleave([stream(i, t) for i in range(rows) for t in range(blocks)], LAG)
    packed = rows_ref[...].astype(BF16)
    for d in range(parties):
        send_ref[d, rows * share :, :] = packed


def second_kernel(
    rows, got_ref, keep_ref, gain_ref, w_ref, gate_bias_ref, w_out_ref, out_bias_ref,
    out_ref, held_ref, bias_ref,
):
    parties = got_ref.shape[0]
    length = keep_ref.shape[1]
    share = length // parties
    blocks = length // LANES
    width = w_ref.shape[2] // 4
    heads = bias_ref.shape[1] // length
    scaling = (width // heads) ** (-0.5) * LOG2E
    held_ref[...] = got_ref[:, : rows * share, :].astype(F32).reshape(held_ref.shape)
    for h in range(heads):
        for t in range(blocks):
            at = rows * share + (t * heads + h) * rows
            turned = got_ref[:, at : at + rows, :].astype(F32).reshape(length, LANES)
            bias_ref[t * LANES : (t + 1) * LANES, h * length : (h + 1) * length] = turned.T * LOG2E
    down, across = head_masks(heads, width)
    w = w_ref[0]
    w_keys = w[:, width : 2 * width].T

    def stream(j):
        x = held_ref[pl.ds(j, length, stride=share), :]
        shifted = x - jnp.mean(x, axis=-1, keepdims=True)
        yield
        spread = jnp.mean(shifted * shifted, axis=-1, keepdims=True)
        yield
        x = (shifted * lax.rsqrt(spread + 1e-05) * gain_ref[1:2, :]).astype(BF16)
        q = (dot(x, w[:, :width]) * scaling).astype(BF16)
        kt = dot(w_keys, x, ((1,), (1,))).astype(BF16)
        yield
        v = dot(x, w[:, 2 * width : 3 * width]).astype(BF16)
        g = jax.nn.sigmoid(dot(x, w[:, 3 * width :]) + gate_bias_ref[1:2, :])
        yield
        for t in range(blocks):
            span = slice(t * LANES, (t + 1) * LANES)
            kept = jnp.broadcast_to(keep_ref[j : j + 1, :], (LANES, length)) > 0
            both = None
            for picked in pairs_of(heads):
                weights = []
                scores = dot(q[span], key_block(kt, picked, down))
                for n, h in enumerate(picked):
                    at = slice(h * length, (h + 1) * length)
                    part = scores[:, n * length : (n + 1) * length]
                    weights.append(softened(part + bias_ref[span, at], kept))
                    yield
                term = dot(jnp.concatenate(weights, axis=1), value_block(v, picked, across))
                both = term if both is None else both + term
                yield
            joined = (g[span] * (both[:, :width] / both[:, width:])).astype(BF16)
            update = dot(joined, w_out_ref[0]) + out_bias_ref[1:2, :]
            at = pl.ds(t * LANES * share + j, LANES, stride=share)
            out_ref[at, :] = held_ref[at, :] + update
            yield

    interleave([stream(j) for j in range(share)], LAG)


LAG = 3


def of_pass(array, p):
    shape = (1,) + array.shape[1:]
    return pl.BlockSpec(shape, lambda *_: (p,) + (0,) * (len(shape) - 1))


SMEM = pl.BlockSpec(memory_space=pltpu.SMEM)


def params():
    return pltpu.CompilerParams(vmem_limit_bytes=VMEM_BYTES)


def local(parties, pair_rep, token_mask, ln_gain, w_proj, w_tri, gate_bias, w_out, out_bias):
    rows, length, channels = pair_rep.shape
    heads = w_tri.shape[2]
    width = w_proj.shape[2] // 4
    share = length // parties
    bias_rows = length // LANES * heads * rows
    early = rows * length * heads * length * 4 <= EARLY_BYTES
    mask = token_mask.reshape(1, length)
    w_tri = jnp.swapaxes(w_tri, 1, 2)
    shape = jax.ShapeDtypeStruct

    def full(array):
        return pl.BlockSpec(array.shape, lambda *_: (0,) * array.ndim)

    send, norm = pl.pallas_call(
        bias_kernel,
        grid=(1,),
        out_shape=(
            shape((parties, bias_rows, LANES), BF16),
            shape((rows, length, channels), BF16),
        ),
        in_specs=[pl.BlockSpec(memory_space=pltpu.HBM), full(ln_gain), of_pass(w_tri, 0)],
        scratch_shapes=[
            pltpu.VMEM((bias_rows, LANES), F32),
            pltpu.VMEM(pair_rep.shape, F32),
            pltpu.SemaphoreType.DMA((rows,)),
        ],
        compiler_params=params(),
        name="bias",
    )(pair_rep, ln_gain, w_tri)
    got = lax.all_to_all(send, "row", split_axis=0, concat_axis=0, tiled=True)
    q, k, v, g, keep, *scores = pl.pallas_call(
        functools.partial(project_kernel, heads, early),
        grid=(1,),
        out_shape=(
            shape((rows, length, width), BF16),
            shape((rows, width, length), BF16),
            shape((rows, length, width), BF16),
            shape((rows, length, width), F32),
            shape((rows, length), jnp.int32),
        )
        + ((shape((rows, length, heads * length), F32),) if early else ()),
        in_specs=[full(norm), SMEM, full(mask), of_pass(w_proj, 0), full(gate_bias)],
        compiler_params=params(),
        cost_estimate=pl.CostEstimate(
            flops=2 * rows * length * channels * 4 * width,
            transcendentals=rows * length * width,
            bytes_accessed=rows * length * width * 12,
        ),
        name="project",
    )(norm, token_mask, mask, w_proj, gate_bias)
    taken = (pair_rep, q, k, v, g, got, keep, ln_gain)
    send = pl.pallas_call(
        functools.partial(first_kernel, early),
        grid=(1,),
        out_shape=shape((parties, rows * share + bias_rows, LANES), BF16),
        in_specs=[full(a) for a in taken]
        + [of_pass(w_tri, 1), of_pass(w_out, 0), full(out_bias)]
        + [full(a) for a in scores],
        scratch_shapes=[
            pltpu.VMEM((length, heads * length), F32),
            pltpu.VMEM((bias_rows, LANES), F32),
        ],
        compiler_params=params(),
        name="first",
    )(*taken, w_tri, w_out, out_bias, *scores)
    got = lax.all_to_all(send, "row", split_axis=0, concat_axis=0, tiled=True)
    out = pl.pallas_call(
        functools.partial(second_kernel, rows),
        grid=(1,),
        out_shape=shape((length * share, channels), F32),
        in_specs=[
            full(got), full(keep), full(ln_gain), of_pass(w_proj, 1), full(gate_bias), of_pass(w_out, 1),
            full(out_bias),
        ],
        scratch_shapes=[
            pltpu.VMEM((length * share, channels), F32),
            pltpu.VMEM((length, heads * length), F32),
        ],
        compiler_params=params(),
        name="second",
    )(got, keep, ln_gain, w_proj, gate_bias, w_out, out_bias)
    return out.reshape(length, share, channels)


def solution(mesh):
    return jax.shard_map(
        functools.partial(local, mesh.shape["row"]),
        mesh=mesh,
        in_specs=(P(("group", "row"), None, None), P("group"), P(), P(), P(), P(), P(), P()),
        out_specs=P("group", "row", None),
        check_vma=False,
    )
```

```python
import functools

import jax
import jax.numpy as jnp
from jax import lax
from jax.experimental import pallas as pl
from jax.experimental.pallas import tpu as pltpu
from jax.sharding import PartitionSpec as P

LANES = 128
VMEM_BYTES = 24 * 2**20
EARLY_BYTES = 0
KEPT = 3
ALL_BYTES = 67 * 10**6
F32 = jnp.float32
BF16 = jnp.bfloat16
MASKED = -1000000000.0
LOG2E = 1.4426950408889634


def dot(a, b, dims=((1,), (0,))):
    return lax.dot_general(a, b, (dims, ((), ())), preferred_element_type=F32)


def interleave(streams, lag):
    waiting = [(i * lag, stream) for i, stream in enumerate(streams)]
    turn = 0
    while waiting:
        left = []
        for start, stream in waiting:
            if start <= turn and next(stream, waiting) is waiting:
                continue
            left.append((start, stream))
        waiting = left
        turn += 1


def normed(x, gain):
    centre = jnp.mean(x, axis=-1, keepdims=True)
    shifted = x - centre
    spread = jnp.mean(shifted * shifted, axis=-1, keepdims=True)
    return (shifted * lax.rsqrt(spread + 1e-05) * gain).astype(BF16)


def head_masks(heads, width):
    dim = width // heads
    down = lax.broadcasted_iota(jnp.int32, (width, LANES), 0) // dim
    across = lax.broadcasted_iota(jnp.int32, (LANES, width), 1) // dim
    return (
        [(down == h).astype(F32).astype(BF16) for h in range(heads)],
        [(across == h).astype(F32).astype(BF16) for h in range(heads)],
    )


def key_block(kt, picked, down):
    spread = []
    for h in picked:
        for t in range(kt.shape[1] // LANES):
            spread.append(kt[:, t * LANES : (t + 1) * LANES] * down[h])
    return jnp.concatenate(spread, axis=1)


def value_block(v, picked, across):
    parts = []
    for h in picked:
        for t in range(v.shape[0] // LANES):
            piece = v[t * LANES : (t + 1) * LANES] * across[h]
            parts.append(jnp.concatenate([piece, across[h]], axis=1))
    return jnp.concatenate(parts, axis=0)


def softened(scores, kept):
    part = jnp.where(kept, scores, F32(MASKED))
    return jnp.exp2(part - jnp.max(part, axis=1, keepdims=True)).astype(BF16)


def pairs_of(heads):
    return [tuple(range(h, min(h + 2, heads))) for h in range(0, heads, 2)]


def bias_kernel(x_ref, gain_ref, w_tri_ref, send_ref, norm_ref, rows_ref, held_ref, sems):
    rows, length, _ = x_ref.shape
    heads = w_tri_ref.shape[1]
    copies = [pltpu.make_async_copy(x_ref.at[i], held_ref.at[i], sems.at[i]) for i in range(rows)]
    for copy in copies:
        copy.start()

    def stream(i, t):
        span = slice(t * LANES, (t + 1) * LANES)
        if t == 0:
            copies[i].wait()
        x = held_ref[i, span, :]
        shifted = x - jnp.mean(x, axis=-1, keepdims=True)
        yield
        spread = jnp.mean(shifted * shifted, axis=-1, keepdims=True)
        yield
        x = (shifted * lax.rsqrt(spread + 1e-05) * gain_ref[0:1, :]).astype(BF16)
        norm_ref[i, span, :] = x
        yield
        rows_ref[pl.ds(t * heads * rows + i, heads, stride=rows), :] = dot(w_tri_ref[0], x, ((1,), (1,)))

    interleave([stream(i, t) for i in range(rows) for t in range(length // LANES)], 1)
    packed = rows_ref[...].astype(BF16)
    for d in range(send_ref.shape[0]):
        send_ref[d] = packed


def project_kernel(heads, early, norm_ref, flag_ref, mask_ref, w_ref, gate_bias_ref, *more_refs):
    out_refs = more_refs[KEPT:]
    q_ref, k_ref, v_ref, g_ref, keep_ref = out_refs[:5]
    rows, length, width = q_ref.shape
    scaling = (width // heads) ** (-0.5)
    down, _ = head_masks(heads, width)
    w = w_ref[0]
    w_keys = w[:, width : 2 * width].T
    first = lax.axis_index("row") * rows

    def stream(i):
        x = norm_ref[i]
        q = (dot(x, w[:, :width]) * scaling).astype(BF16)
        q_ref[i] = q
        kt = dot(w_keys, x, ((1,), (1,))).astype(BF16)
        k_ref[i] = kt
        yield
        v_ref[i] = dot(x, w[:, 2 * width : 3 * width]).astype(BF16)
        g_ref[i] = jax.nn.sigmoid(dot(x, w[:, 3 * width :]) + gate_bias_ref[0:1, :])
        keep_ref[i : i + 1, :] = mask_ref[...] * flag_ref[first + i]
        yield
        if early:
            for picked in pairs_of(heads):
                at = slice(picked[0] * length, (picked[-1] + 1) * length)
                out_refs[5][i, :, at] = dot(q, key_block(kt, picked, down)) * LOG2E
                yield

    interleave([stream(i) for i in range(rows)], 2)


def first_kernel(
    early, x_ref, q_ref, k_ref, v_ref, g_ref, got_ref, keep_ref, gain_ref, w_tri_ref, w_out_ref, out_bias_ref,
    *more_refs,
):
    send_ref, bias_ref, rows_ref = more_refs[-3:]
    rows, length, width = q_ref.shape
    heads = w_tri_ref.shape[1]
    parties = send_ref.shape[0]
    share = length // parties
    blocks = length // LANES
    for h in range(heads):
        for t in range(blocks):
            at = (t * heads + h) * rows
            bias_ref[:, h * length + t * LANES : h * length + (t + 1) * LANES] = (
                got_ref[:, at : at + rows, :].astype(F32).reshape(length, LANES) * LOG2E
            )
    down, across = head_masks(heads, width)

    def stream(i, t):
        span = slice(t * LANES, (t + 1) * LANES)
        kept = jnp.broadcast_to(keep_ref[i : i + 1, :], (LANES, length)) > 0
        both = None
        for picked in pairs_of(heads):
            weights = []
            scores = None
            if not early:
                scores = dot(q_ref[i, span, :], key_block(k_ref[i], picked, down)) * LOG2E
            for n, h in enumerate(picked):
                at = slice(h * length, (h + 1) * length)
                part = more_refs[0][i, span, at] if early else scores[:, n * length : (n + 1) * length]
                weights.append(softened(part + bias_ref[span, at], kept))
                yield
            term = dot(jnp.concatenate(weights, axis=1), value_block(v_ref[i], picked, across))
            both = term if both is None else both + term
            yield
        joined = (g_ref[i, span, :] * (both[:, :width] / both[:, width:])).astype(BF16)
        stacked = x_ref[i, span, :] + (dot(joined, w_out_ref[0]) + out_bias_ref[0:1, :])
        reach = LANES // share
        send_ref[t * reach : (t + 1) * reach, i * share : (i + 1) * share, :] = stacked.reshape(
            reach, share, stacked.shape[1]
        ).astype(BF16)
        yield
        shifted = stacked - jnp.mean(stacked, axis=-1, keepdims=True)
        yield
        spread = jnp.mean(shifted * shifted, axis=-1, keepdims=True)
        yield
        x = (shifted * lax.rsqrt(spread + 1e-05) * gain_ref[1:2, :]).astype(BF16)
        rows_ref[pl.ds(t * heads * rows + i, heads, stride=rows), :] = dot(w_tri_ref[0], x, ((1,), (1,)))

    interleave([stream(i, t) for i in range(rows) for t in range(blocks)], LAG)
    packed = rows_ref[...].astype(BF16)
    for d in range(parties):
        send_ref[d, rows * share :, :] = packed


def second_kernel(
    rows, got_ref, keep_ref, gain_ref, w_ref, gate_bias_ref, w_out_ref, out_bias_ref,
    out_ref, held_ref, bias_ref,
):
    parties = got_ref.shape[0]
    length = keep_ref.shape[1]
    share = length // parties
    blocks = length // LANES
    width = w_ref.shape[2] // 4
    heads = bias_ref.shape[1] // length
    scaling = (width // heads) ** (-0.5) * LOG2E
    held_ref[...] = got_ref[:, : rows * share, :].astype(F32).reshape(held_ref.shape)
    for h in range(heads):
        for t in range(blocks):
            at = rows * share + (t * heads + h) * rows
            turned = got_ref[:, at : at + rows, :].astype(F32).reshape(length, LANES)
            bias_ref[t * LANES : (t + 1) * LANES, h * length : (h + 1) * length] = turned.T * LOG2E
    down, across = head_masks(heads, width)
    w = w_ref[0]
    w_keys = w[:, width : 2 * width].T

    def stream(j):
        x = held_ref[pl.ds(j, length, stride=share), :]
        shifted = x - jnp.mean(x, axis=-1, keepdims=True)
        yield
        spread = jnp.mean(shifted * shifted, axis=-1, keepdims=True)
        yield
        x = (shifted * lax.rsqrt(spread + 1e-05) * gain_ref[1:2, :]).astype(BF16)
        q = (dot(x, w[:, :width]) * scaling).astype(BF16)
        kt = dot(w_keys, x, ((1,), (1,))).astype(BF16)
        yield
        v = dot(x, w[:, 2 * width : 3 * width]).astype(BF16)
        g = jax.nn.sigmoid(dot(x, w[:, 3 * width :]) + gate_bias_ref[1:2, :])
        yield
        for t in range(blocks):
            span = slice(t * LANES, (t + 1) * LANES)
            kept = jnp.broadcast_to(keep_ref[j : j + 1, :], (LANES, length)) > 0
            both = None
            for picked in pairs_of(heads):
                weights = []
                scores = dot(q[span], key_block(kt, picked, down))
                for n, h in enumerate(picked):
                    at = slice(h * length, (h + 1) * length)
                    part = scores[:, n * length : (n + 1) * length]
                    weights.append(softened(part + bias_ref[span, at], kept))
                    yield
                term = dot(jnp.concatenate(weights, axis=1), value_block(v, picked, across))
                both = term if both is None else both + term
                yield
            joined = (g[span] * (both[:, :width] / both[:, width:])).astype(BF16)
            update = dot(joined, w_out_ref[0]) + out_bias_ref[1:2, :]
            at = pl.ds(t * LANES * share + j, LANES, stride=share)
            out_ref[at, :] = held_ref[at, :] + update
            yield

    interleave([stream(j) for j in range(share)], LAG)


LAG = 1


def of_pass(array, p):
    shape = (1,) + array.shape[1:]
    return pl.BlockSpec(shape, lambda *_: (p,) + (0,) * (len(shape) - 1))


SMEM = pl.BlockSpec(memory_space=pltpu.SMEM)


def params(limit=VMEM_BYTES):
    return pltpu.CompilerParams(vmem_limit_bytes=limit)


def local(parties, pair_rep, token_mask, ln_gain, w_proj, w_tri, gate_bias, w_out, out_bias):
    rows, length, channels = pair_rep.shape
    heads = w_tri.shape[2]
    width = w_proj.shape[2] // 4
    share = length // parties
    bias_rows = length // LANES * heads * rows
    early = rows * length * heads * length * 4 <= EARLY_BYTES
    mask = token_mask.reshape(1, length)
    w_tri = jnp.swapaxes(w_tri, 1, 2)
    shape = jax.ShapeDtypeStruct

    def full(array):
        return pl.BlockSpec(array.shape, lambda *_: (0,) * array.ndim)

    send, norm = pl.pallas_call(
        bias_kernel,
        grid=(1,),
        out_shape=(
            shape((parties, bias_rows, LANES), BF16),
            shape((rows, length, channels), BF16),
        ),
        in_specs=[pl.BlockSpec(memory_space=pltpu.HBM), full(ln_gain), of_pass(w_tri, 0)],
        scratch_shapes=[
            pltpu.VMEM((bias_rows, LANES), F32),
            pltpu.VMEM(pair_rep.shape, F32),
            pltpu.SemaphoreType.DMA((rows,)),
        ],
        compiler_params=params(ALL_BYTES),
        name="bias",
    )(pair_rep, ln_gain, w_tri)
    got = lax.all_to_all(send, "row", split_axis=0, concat_axis=0, tiled=True)
    kept = (w_tri, ln_gain, out_bias)
    q, k, v, g, keep, *scores = pl.pallas_call(
        functools.partial(project_kernel, heads, early),
        grid=(1,),
        out_shape=(
            shape((rows, length, width), BF16),
            shape((rows, width, length), BF16),
            shape((rows, length, width), BF16),
            shape((rows, length, width), F32),
            shape((rows, length), jnp.int32),
        )
        + ((shape((rows, length, heads * length), F32),) if early else ()),
        in_specs=[full(norm), SMEM, full(mask), of_pass(w_proj, 0), full(gate_bias)] + [full(a) for a in kept],
        compiler_params=params(),
        cost_estimate=pl.CostEstimate(
            flops=2 * rows * length * channels * 4 * width,
            transcendentals=rows * length * width,
            bytes_accessed=rows * length * width * 12,
        ),
        name="project",
    )(norm, token_mask, mask, w_proj, gate_bias, *kept)
    taken = (pair_rep, q, k, v, g, got, keep, ln_gain)
    send = pl.pallas_call(
        functools.partial(first_kernel, early),
        grid=(1,),
        out_shape=shape((parties, rows * share + bias_rows, LANES), BF16),
        in_specs=[full(a) for a in taken]
        + [of_pass(w_tri, 1), of_pass(w_out, 0), full(out_bias)]
        + [full(a) for a in scores],
        scratch_shapes=[
            pltpu.VMEM((length, heads * length), F32),
            pltpu.VMEM((bias_rows, LANES), F32),
        ],
        compiler_params=params(),
        name="first",
    )(*taken, w_tri, w_out, out_bias, *scores)
    got = lax.all_to_all(send, "row", split_axis=0, concat_axis=0, tiled=True)
    out = pl.pallas_call(
        functools.partial(second_kernel, rows),
        grid=(1,),
        out_shape=shape((length * share, channels), F32),
        in_specs=[
            full(got), full(keep), full(ln_gain), of_pass(w_proj, 1), full(gate_bias), of_pass(w_out, 1),
            full(out_bias),
        ],
        scratch_shapes=[
            pltpu.VMEM((length * share, channels), F32),
            pltpu.VMEM((length, heads * length), F32),
        ],
        compiler_params=params(),
        name="second",
    )(got, keep, ln_gain, w_proj, gate_bias, w_out, out_bias)
    return out.reshape(length, share, channels)


def solution(mesh):
    return jax.shard_map(
        functools.partial(local, mesh.shape["row"]),
        mesh=mesh,
        in_specs=(P(("group", "row"), None, None), P("group"), P(), P(), P(), P(), P(), P()),
        out_specs=P("group", "row", None),
        check_vma=False,
    )
```

```python
import functools

import jax
import jax.numpy as jnp
from jax import lax
from jax.experimental import pallas as pl
from jax.experimental.pallas import tpu as pltpu
from jax.sharding import PartitionSpec as P

LANES = 128
VMEM_BYTES = 24 * 2**20
KEPT = 2
ALL_BYTES = 67 * 10**6
F32 = jnp.float32
BF16 = jnp.bfloat16
MASKED = -1000000000.0
LOG2E = 1.4426950408889634


def dot(a, b, dims=((1,), (0,))):
    return lax.dot_general(a, b, (dims, ((), ())), preferred_element_type=F32)


def interleave(streams, lag):
    waiting = [(i * lag, stream) for i, stream in enumerate(streams)]
    turn = 0
    while waiting:
        left = []
        for start, stream in waiting:
            if start <= turn and next(stream, waiting) is waiting:
                continue
            left.append((start, stream))
        waiting = left
        turn += 1


def normed(x, gain):
    centre = jnp.mean(x, axis=-1, keepdims=True)
    shifted = x - centre
    spread = jnp.mean(shifted * shifted, axis=-1, keepdims=True)
    return (shifted * lax.rsqrt(spread + 1e-05) * gain).astype(BF16)


def head_masks(heads, width):
    dim = width // heads
    down = lax.broadcasted_iota(jnp.int32, (width, LANES), 0) // dim
    across = lax.broadcasted_iota(jnp.int32, (LANES, width), 1) // dim
    return (
        [(down == h).astype(F32).astype(BF16) for h in range(heads)],
        [(across == h).astype(F32).astype(BF16) for h in range(heads)],
    )


def key_block(kt, picked, down):
    spread = []
    for h in picked:
        for t in range(kt.shape[1] // LANES):
            spread.append(kt[:, t * LANES : (t + 1) * LANES] * down[h])
    return jnp.concatenate(spread, axis=1)


def value_block(v, picked, across):
    parts = []
    for h in picked:
        for t in range(v.shape[0] // LANES):
            piece = v[t * LANES : (t + 1) * LANES] * across[h]
            parts.append(jnp.concatenate([piece, across[h]], axis=1))
    return jnp.concatenate(parts, axis=0)


def softened(scores, kept):
    part = jnp.where(kept, scores, F32(MASKED))
    return jnp.exp2(part - jnp.max(part, axis=1, keepdims=True)).astype(BF16)


def pairs_of(heads):
    return [tuple(range(h, min(h + 2, heads))) for h in range(0, heads, 2)]


def bias_kernel(x_ref, gain_ref, w_tri_ref, send_ref, rows_ref, held_ref, scale_ref, weight_ref, sems):
    rows, length, _ = x_ref.shape
    heads = w_tri_ref.shape[1]
    copies = [pltpu.make_async_copy(x_ref.at[i], held_ref.at[i], sems.at[i]) for i in range(rows)]
    copies += [
        pltpu.make_async_copy(gain_ref, scale_ref, sems.at[rows]),
        pltpu.make_async_copy(w_tri_ref.at[0], weight_ref, sems.at[rows + 1]),
    ]
    for copy in copies:
        copy.start()
    copies[rows].wait()
    copies[rows + 1].wait()

    def stream(i, t):
        if t == 0:
            copies[i].wait()
        x = held_ref[i, t * LANES : (t + 1) * LANES, :]
        shifted = x - jnp.mean(x, axis=-1, keepdims=True)
        yield
        spread = jnp.mean(shifted * shifted, axis=-1, keepdims=True)
        yield
        x = (shifted * lax.rsqrt(spread + 1e-05) * scale_ref[0:1, :]).astype(BF16)
        yield
        rows_ref[pl.ds(t * heads * rows + i, heads, stride=rows), :] = dot(weight_ref[...], x, ((1,), (1,)))

    interleave([stream(i, t) for i in range(rows) for t in range(length // LANES)], 1)
    packed = rows_ref[...].astype(BF16)
    for d in range(send_ref.shape[0]):
        send_ref[d] = packed


def project_kernel(heads, x_ref, gain_ref, flag_ref, mask_ref, w_ref, gate_bias_ref, *more_refs):
    q_ref, k_ref, v_ref, g_ref, keep_ref = more_refs[KEPT:]
    rows, length, width = q_ref.shape
    scaling = (width // heads) ** (-0.5) * LOG2E
    w = w_ref[0]
    w_keys = w[:, width : 2 * width].T
    first = lax.axis_index("row") * rows

    def stream(i):
        x = x_ref[i]
        shifted = x - jnp.mean(x, axis=-1, keepdims=True)
        yield
        spread = jnp.mean(shifted * shifted, axis=-1, keepdims=True)
        yield
        x = (shifted * lax.rsqrt(spread + 1e-05) * gain_ref[0:1, :]).astype(BF16)
        q_ref[i] = (dot(x, w[:, :width]) * scaling).astype(BF16)
        k_ref[i] = dot(w_keys, x, ((1,), (1,))).astype(BF16)
        yield
        v_ref[i] = dot(x, w[:, 2 * width : 3 * width]).astype(BF16)
        g_ref[i] = jax.nn.sigmoid(dot(x, w[:, 3 * width :]) + gate_bias_ref[0:1, :])
        keep_ref[i : i + 1, :] = mask_ref[...] * flag_ref[first + i]

    interleave([stream(i) for i in range(rows)], 1)


def first_kernel(
    rank, x_ref, q_ref, k_ref, v_ref, g_ref, got_ref, keep_ref, gain_ref, w_tri_ref, w_out_ref, out_bias_ref,
    send_ref, bias_ref, rows_ref,
):
    rows, length, width = q_ref.shape
    heads = w_tri_ref.shape[1]
    parties = send_ref.shape[0]
    share = length // parties
    blocks = length // LANES
    for h in range(heads):
        for t in range(blocks):
            at = (t * heads + h) * rows
            for s in range(parties):
                bias_ref[s * rows : (s + 1) * rows, h * length + t * LANES : h * length + (t + 1) * LANES] = (
                    got_ref[rank[s], at : at + rows, :].astype(F32) * LOG2E
                )
    down, across = head_masks(heads, width)

    def stream(i, t):
        span = slice(t * LANES, (t + 1) * LANES)
        kept = jnp.broadcast_to(keep_ref[i : i + 1, :], (LANES, length)) > 0
        both = None
        for picked in pairs_of(heads):
            weights = []
            scores = dot(q_ref[i, span, :], key_block(k_ref[i], picked, down))
            for n, h in enumerate(picked):
                at = slice(h * length, (h + 1) * length)
                part = scores[:, n * length : (n + 1) * length]
                weights.append(softened(part + bias_ref[span, at], kept))
                yield
            term = dot(jnp.concatenate(weights, axis=1), value_block(v_ref[i], picked, across))
            both = term if both is None else both + term
            yield
        joined = (g_ref[i, span, :] * (both[:, :width] / both[:, width:])).astype(BF16)
        stacked = x_ref[i, span, :] + (dot(joined, w_out_ref[0]) + out_bias_ref[0:1, :])
        reach = LANES // share
        for d in range(reach):
            send_ref[rank[t * reach + d], i * share : (i + 1) * share, :] = stacked[
                d * share : (d + 1) * share
            ].astype(BF16)
        yield
        shifted = stacked - jnp.mean(stacked, axis=-1, keepdims=True)
        yield
        spread = jnp.mean(shifted * shifted, axis=-1, keepdims=True)
        yield
        x = (shifted * lax.rsqrt(spread + 1e-05) * gain_ref[1:2, :]).astype(BF16)
        rows_ref[pl.ds(t * heads * rows + i, heads, stride=rows), :] = dot(w_tri_ref[0], x, ((1,), (1,)))

    interleave([stream(i, t) for i in range(rows) for t in range(blocks)], LAG)
    packed = rows_ref[...].astype(BF16)
    for d in range(parties):
        send_ref[d, rows * share :, :] = packed


def second_kernel(
    rows, rank, got_ref, keep_ref, gain_ref, w_ref, gate_bias_ref, w_out_ref, out_bias_ref,
    out_ref, held_ref, bias_ref,
):
    parties = got_ref.shape[0]
    length = keep_ref.shape[1]
    share = length // parties
    blocks = length // LANES
    width = w_ref.shape[2] // 4
    heads = bias_ref.shape[1] // length
    scaling = (width // heads) ** (-0.5) * LOG2E
    for s in range(parties):
        held_ref[s * rows * share : (s + 1) * rows * share, :] = got_ref[rank[s], : rows * share, :].astype(F32)
    for h in range(heads):
        for t in range(blocks):
            at = rows * share + (t * heads + h) * rows
            turned = jnp.concatenate(
                [got_ref[rank[s], at : at + rows, :].astype(F32) for s in range(parties)], axis=0
            )
            bias_ref[t * LANES : (t + 1) * LANES, h * length : (h + 1) * length] = turned.T * LOG2E
    down, across = head_masks(heads, width)
    w = w_ref[0]
    w_keys = w[:, width : 2 * width].T

    def stream(j):
        x = held_ref[pl.ds(j, length, stride=share), :]
        shifted = x - jnp.mean(x, axis=-1, keepdims=True)
        yield
        spread = jnp.mean(shifted * shifted, axis=-1, keepdims=True)
        yield
        x = (shifted * lax.rsqrt(spread + 1e-05) * gain_ref[1:2, :]).astype(BF16)
        q = (dot(x, w[:, :width]) * scaling).astype(BF16)
        kt = dot(w_keys, x, ((1,), (1,))).astype(BF16)
        yield
        v = dot(x, w[:, 2 * width : 3 * width]).astype(BF16)
        g = jax.nn.sigmoid(dot(x, w[:, 3 * width :]) + gate_bias_ref[1:2, :])
        yield
        for t in range(blocks):
            span = slice(t * LANES, (t + 1) * LANES)
            kept = jnp.broadcast_to(keep_ref[j : j + 1, :], (LANES, length)) > 0
            both = None
            for picked in pairs_of(heads):
                weights = []
                scores = dot(q[span], key_block(kt, picked, down))
                for n, h in enumerate(picked):
                    at = slice(h * length, (h + 1) * length)
                    part = scores[:, n * length : (n + 1) * length]
                    weights.append(softened(part + bias_ref[span, at], kept))
                    yield
                term = dot(jnp.concatenate(weights, axis=1), value_block(v, picked, across))
                both = term if both is None else both + term
                yield
            joined = (g[span] * (both[:, :width] / both[:, width:])).astype(BF16)
            update = dot(joined, w_out_ref[0]) + out_bias_ref[1:2, :]
            at = pl.ds(t * LANES * share + j, LANES, stride=share)
            out_ref[at, :] = held_ref[at, :] + update
            yield

    interleave([stream(j) for j in range(share)], LAG)


LAG = 1


def of_pass(array, p):
    shape = (1,) + array.shape[1:]
    return pl.BlockSpec(shape, lambda *_: (p,) + (0,) * (len(shape) - 1))


SMEM = pl.BlockSpec(memory_space=pltpu.SMEM)


def group_order(parties):
    stride = max(parties // 4, 1)
    middle = [2, 1, 3, 0]
    order = [m * stride + k for k in range(stride) for m in middle if m * stride + k < parties]
    lead = parties // 2 + (1 if parties > 2 else 0)
    return [lead] + [d for d in order if d != lead]


def params(limit=VMEM_BYTES):
    return pltpu.CompilerParams(vmem_limit_bytes=limit)


def local(parties, pair_rep, token_mask, ln_gain, w_proj, w_tri, gate_bias, w_out, out_bias):
    rows, length, channels = pair_rep.shape
    heads = w_tri.shape[2]
    width = w_proj.shape[2] // 4
    share = length // parties
    bias_rows = length // LANES * heads * rows
    mask = token_mask.reshape(1, length)
    w_tri = jnp.swapaxes(w_tri, 1, 2)
    shape = jax.ShapeDtypeStruct

    def full(array):
        return pl.BlockSpec(array.shape, lambda *_: (0,) * array.ndim)

    order = group_order(parties)
    rank = [order.index(d) for d in range(parties)]

    def exchange(parts):
        return lax.all_to_all(parts, "row", split_axis=0, concat_axis=0, tiled=True, axis_index_groups=[order])

    hbm = pl.BlockSpec(memory_space=pltpu.HBM)
    send = pl.pallas_call(
        bias_kernel,
        grid=(1,),
        out_shape=shape((parties, bias_rows, LANES), BF16),
        in_specs=[hbm, hbm, hbm],
        scratch_shapes=[
            pltpu.VMEM((bias_rows, LANES), F32),
            pltpu.VMEM(pair_rep.shape, F32),
            pltpu.VMEM(ln_gain.shape, F32),
            pltpu.VMEM(w_tri.shape[1:], BF16),
            pltpu.SemaphoreType.DMA((rows + 2,)),
        ],
        compiler_params=params(ALL_BYTES),
        name="bias",
    )(pair_rep, ln_gain, w_tri)
    got = exchange(send)
    kept = (w_tri, out_bias)
    q, k, v, g, keep = pl.pallas_call(
        functools.partial(project_kernel, heads),
        grid=(1,),
        out_shape=(
            shape((rows, length, width), BF16),
            shape((rows, width, length), BF16),
            shape((rows, length, width), BF16),
            shape((rows, length, width), F32),
            shape((rows, length), jnp.int32),
        ),
        in_specs=[full(pair_rep), full(ln_gain), SMEM, full(mask), of_pass(w_proj, 0), full(gate_bias)]
        + [full(a) for a in kept],
        compiler_params=params(),
        cost_estimate=pl.CostEstimate(
            flops=2 * rows * length * channels * 4 * width,
            transcendentals=rows * length * width,
            bytes_accessed=rows * length * width * 12,
        ),
        name="project",
    )(pair_rep, ln_gain, token_mask, mask, w_proj, gate_bias, *kept)
    taken = (pair_rep, q, k, v, g, got, keep, ln_gain)
    send = pl.pallas_call(
        functools.partial(first_kernel, rank),
        grid=(1,),
        out_shape=shape((parties, rows * share + bias_rows, LANES), BF16),
        in_specs=[full(a) for a in taken]
        + [of_pass(w_tri, 1), of_pass(w_out, 0), full(out_bias)],
        scratch_shapes=[
            pltpu.VMEM((length, heads * length), F32),
            pltpu.VMEM((bias_rows, LANES), F32),
        ],
        compiler_params=params(),
        name="first",
    )(*taken, w_tri, w_out, out_bias)
    got = exchange(send)
    out = pl.pallas_call(
        functools.partial(second_kernel, rows, rank),
        grid=(1,),
        out_shape=shape((length * share, channels), F32),
        in_specs=[
            full(got), full(keep), full(ln_gain), of_pass(w_proj, 1), full(gate_bias), of_pass(w_out, 1),
            full(out_bias),
        ],
        scratch_shapes=[
            pltpu.VMEM((length * share, channels), F32),
            pltpu.VMEM((length, heads * length), F32),
        ],
        compiler_params=params(),
        name="second",
    )(got, keep, ln_gain, w_proj, gate_bias, w_out, out_bias)
    return out.reshape(length, share, channels)


def solution(mesh):
    return jax.shard_map(
        functools.partial(local, mesh.shape["row"]),
        mesh=mesh,
        in_specs=(P(("group", "row"), None, None), P("group"), P(), P(), P(), P(), P(), P()),
        out_specs=P("group", "row", None),
        check_vma=False,
    )
```

```python
import functools

import jax
import jax.numpy as jnp
from jax import lax
from jax.experimental import pallas as pl
from jax.experimental.pallas import tpu as pltpu
from jax.sharding import PartitionSpec as P

LANES = 128
VMEM_BYTES = 24 * 2**20
KEPT = 2
PIECE = 32
TOKENS = 1024
F32 = jnp.float32
BF16 = jnp.bfloat16
MASKED = -1000000000.0
EPSILON = 1e-05
LOG2E = 1.4426950408889634


def dot(a, b, dims=((1,), (0,))):
    return lax.dot_general(a, b, (dims, ((), ())), preferred_element_type=F32)


def in_step(streams, together):
    streams = list(streams)
    for at in range(0, len(streams), together):
        group = streams[at : at + together]
        while group:
            group = [stream for stream in group if next(stream, group) is not group]


def own_rows(turned, h, heads):
    width, n = turned.shape
    dim = width // heads
    parts = [turned[h * dim : (h + 1) * dim]]
    if h:
        parts.insert(0, jnp.zeros((h * dim, n), turned.dtype))
    if h < heads - 1:
        parts.append(jnp.zeros((width - (h + 1) * dim, n), turned.dtype))
    return jnp.concatenate(parts, axis=0)


def query_block(qt, picked, heads):
    return jnp.concatenate([own_rows(qt, h, heads) for h in picked], axis=1)


def attention(k, qt, vt, gt, bias, lift, heads, result):
    dim = vt.shape[0] // heads
    weights = []
    for picked in pairs_of(heads):
        scores = dot(k, query_block(qt, picked, heads))
        for n, h in enumerate(picked):
            part = scores[:, n * LANES : (n + 1) * LANES] + bias(h)
            part = jnp.exp2(part - jnp.max(part, axis=0, keepdims=True)).astype(BF16)
            weights.append(jnp.maximum(part, lift))
            yield
    ones = jnp.ones((16, vt.shape[1]), BF16)
    mixture = []
    for picked in pairs_of(heads):
        rows = jnp.concatenate([vt[h * dim : (h + 1) * dim] for h in picked] + [ones], axis=0)
        both = dot(rows, jnp.concatenate([weights[h] for h in picked], axis=1))
        for n, h in enumerate(picked):
            column = both[:, n * LANES : (n + 1) * LANES]
            mixture.append(column[n * dim : (n + 1) * dim] * (1.0 / column[len(picked) * dim : len(picked) * dim + 1]))
        yield
    result.append((gt * jnp.concatenate(mixture, axis=0)).astype(BF16))


def turned_weights(w, width):
    sides = [w[:, at * width : (at + 1) * width] for at in (0, 2, 3)]
    return jnp.concatenate([side.T for side in sides], axis=0), w[:, width : 2 * width]


def gate_column(row, length):
    column = jnp.broadcast_to(row, (LANES, row.shape[1])).T
    return jnp.concatenate([column] * (length // LANES), axis=1)


def lift_of(row, length):
    return jnp.broadcast_to(row, (length, LANES)).astype(BF16)


def masked(part, column):
    return jnp.where(column > 0, part * LOG2E, F32(MASKED))


def projected(x, sides, keys, gate, scaling):
    width = keys.shape[1]
    three = dot(sides, x, ((1,), (1,)))
    qt = (three[:width] * scaling).astype(BF16)
    vt = three[width : 2 * width].astype(BF16)
    gt = jax.nn.sigmoid(three[2 * width :] + gate)
    return qt, dot(x, keys).astype(BF16), vt, gt


def pairs_of(heads):
    return [tuple(range(h, min(h + 2, heads))) for h in range(0, heads, 2)]


def bias_kernel(x_ref, gain_ref, w_tri_ref, send_ref, rows_ref, held_ref, scale_ref, weight_ref, sems):
    rows, length, _ = x_ref.shape
    heads = w_tri_ref.shape[1]
    copies = [
        pltpu.make_async_copy(x_ref, held_ref, sems.at[0]),
        pltpu.make_async_copy(gain_ref, scale_ref, sems.at[1]),
        pltpu.make_async_copy(w_tri_ref.at[0], weight_ref, sems.at[2]),
    ]
    for copy in copies:
        copy.start()
    for copy in copies:
        copy.wait()

    scale = scale_ref[0:1, :] * held_ref.shape[2] ** 0.5

    def stream(i, t):
        x = held_ref[i, t * LANES : (t + 1) * LANES, :]
        shifted = x - jnp.mean(x, axis=-1, keepdims=True)
        yield
        spread = jnp.sum(shifted * shifted, axis=-1, keepdims=True)
        yield
        x = (shifted * lax.rsqrt(spread + EPSILON * x.shape[1]) * scale).astype(BF16)
        yield
        rows_ref[pl.ds(t * heads * rows + i, heads, stride=rows), :] = dot(weight_ref[...], x, ((1,), (1,)))

    in_step((stream(i, t) for i in range(rows) for t in range(length // LANES)), max(TOKENS // length, 1))
    packed = rows_ref[...].astype(BF16)
    for d in range(send_ref.shape[0]):
        send_ref[d] = packed


def project_kernel(heads, x_ref, gain_ref, flag_ref, mask_ref, w_ref, gate_bias_ref, *more_refs):
    q_ref, k_ref, v_ref, g_ref, column_ref, lift_ref = more_refs[KEPT:]
    rows, length, width = k_ref.shape
    scaling = (width // heads) ** (-0.5) * LOG2E
    sides, keys = turned_weights(w_ref[0], width)
    gate = gate_column(gate_bias_ref[0:1, :], length)
    first = lax.axis_index("row") * rows
    for i in range(rows):
        lift_ref[i : i + 1, :] = jnp.full((1, LANES), jnp.where(flag_ref[first + i] > 0, F32(0.0), F32(1.0)))
    column_ref[...] = jnp.broadcast_to((mask_ref[...] > 0).astype(F32), (LANES, length)).T
    gain = gain_ref[0:1, :] * x_ref.shape[2] ** 0.5

    def stream(i):
        x = x_ref[i]
        shifted = x - jnp.mean(x, axis=-1, keepdims=True)
        yield
        spread = jnp.sum(shifted * shifted, axis=-1, keepdims=True)
        yield
        x = (shifted * lax.rsqrt(spread + EPSILON * x.shape[1]) * gain).astype(BF16)
        q_ref[i], k_ref[i], v_ref[i], g_ref[i] = projected(x, sides, keys, gate, scaling)

    in_step((stream(i) for i in range(rows)), max(TOKENS // length, 1))


def first_kernel(
    rank, rank_out, x_ref, q_ref, k_ref, v_ref, g_ref, got_ref, column_ref, lift_ref, gain_ref, w_tri_ref, w_out_ref,
    out_bias_ref, send_ref, bias_ref, rows_ref,
):
    rows, length, width = k_ref.shape
    heads = w_tri_ref.shape[1]
    parties = send_ref.shape[0]
    share = length // parties
    blocks = length // LANES
    reach = LANES // share
    for h in range(heads):
        for t in range(blocks):
            at = (t * heads + h) * rows
            for b in range(blocks):
                part = jnp.concatenate(
                    [got_ref[rank[s], at : at + rows, :].astype(F32) for s in range(b * reach, (b + 1) * reach)], axis=0
                )
                span = slice(t * LANES, (t + 1) * LANES)
                bias_ref[span, (b * heads + h) * LANES : (b * heads + h + 1) * LANES] = masked(
                    part.T, column_ref[span, :]
                )
    gain = gain_ref[1:2, :] * x_ref.shape[2] ** 0.5

    def stream(i, t):
        span = slice(t * LANES, (t + 1) * LANES)
        lift = lift_of(lift_ref[i : i + 1, :], length)
        result = []

        def bias(h):
            return bias_ref[:, (t * heads + h) * LANES : (t * heads + h + 1) * LANES]

        yield from attention(
            k_ref[i], q_ref[i, :, span], v_ref[i], g_ref[i, :, span], bias, lift, heads, result
        )
        stacked = x_ref[i, span, :] + (dot(result[0], w_out_ref[0], ((0,), (0,))) + out_bias_ref[0:1, :])
        for d in range(reach):
            send_ref[rank_out[t * reach + d], i * share : (i + 1) * share, :] = stacked[
                d * share : (d + 1) * share
            ].astype(BF16)
        yield
        shifted = stacked - jnp.mean(stacked, axis=-1, keepdims=True)
        yield
        spread = jnp.sum(shifted * shifted, axis=-1, keepdims=True)
        yield
        x = (shifted * lax.rsqrt(spread + EPSILON * stacked.shape[1]) * gain).astype(BF16)
        rows_ref[pl.ds(t * heads * rows + i, heads, stride=rows), :] = dot(w_tri_ref[0], x, ((1,), (1,)))

    in_step((stream(i, t) for i in range(rows) for t in range(blocks)), max(TOKENS // length, 1))
    packed = rows_ref[...].astype(BF16)
    for d in range(parties):
        send_ref[d, rows * share :, :] = packed


def second_kernel(
    rows, rank, got_ref, column_ref, lift_ref, gain_ref, w_ref, gate_bias_ref, w_out_ref, out_bias_ref,
    out_ref, held_ref, bias_ref, sems,
):
    parties = got_ref.shape[0]
    length = column_ref.shape[0]
    share = length // parties
    blocks = length // LANES
    width = w_ref.shape[2] // 4
    heads = bias_ref.shape[1] // length
    scaling = (width // heads) ** (-0.5) * LOG2E
    for s in range(parties):
        held_ref[s * rows * share : (s + 1) * rows * share, :] = got_ref[rank[s], : rows * share, :].astype(F32)
    for n in range(heads * blocks):
        at = rows * share + n * rows
        for s in range(parties):
            span = slice(s * rows, (s + 1) * rows)
            bias_ref[span, n * LANES : (n + 1) * LANES] = masked(
                got_ref[rank[s], at : at + rows, :].astype(F32), column_ref[span, :]
            )
    sides, keys = turned_weights(w_ref[0], width)
    gate = gate_column(gate_bias_ref[1:2, :], length)
    gain = gain_ref[1:2, :] * held_ref.shape[1] ** 0.5

    def piece(n):
        at = pl.ds(n * PIECE * share, PIECE * share)
        return pltpu.make_async_copy(held_ref.at[at], out_ref.at[at], sems.at[n])

    copies = [piece(n) for n in range(length // PIECE)]
    stored = [0] * len(copies)
    sent = [0]

    def stream(j):
        x = held_ref[pl.ds(j, length, stride=share), :]
        shifted = x - jnp.mean(x, axis=-1, keepdims=True)
        yield
        spread = jnp.sum(shifted * shifted, axis=-1, keepdims=True)
        yield
        x = (shifted * lax.rsqrt(spread + EPSILON * x.shape[1]) * gain).astype(BF16)
        qt, k, vt, gt = projected(x, sides, keys, gate, scaling)
        yield
        lift = lift_of(lift_ref[j : j + 1, :], length)
        for t in range(blocks):
            span = slice(t * LANES, (t + 1) * LANES)
            result = []

            def bias(h, t=t):
                return bias_ref[:, (t * heads + h) * LANES : (t * heads + h + 1) * LANES]

            yield from attention(k, qt[:, span], vt, gt[:, span], bias, lift, heads, result)
            update = dot(result[0], w_out_ref[0], ((0,), (0,))) + out_bias_ref[1:2, :]
            yield
            for p in range(LANES // PIECE):
                at = pl.ds((t * LANES + p * PIECE) * share + j, PIECE, stride=share)
                held_ref[at, :] = held_ref[at, :] + update[p * PIECE : (p + 1) * PIECE]
                stored[t * (LANES // PIECE) + p] += 1
                while sent[0] < len(copies) and stored[min(sent[0] + 1, len(copies) - 1)] == share:
                    copies[sent[0]].start()
                    sent[0] += 1
                yield

    in_step((stream(j) for j in range(share)), max(TOKENS // length, 1))
    for copy in copies:
        copy.wait()


def of_pass(array, p):
    shape = (1,) + array.shape[1:]
    return pl.BlockSpec(shape, lambda *_: (p,) + (0,) * (len(shape) - 1))


SMEM = pl.BlockSpec(memory_space=pltpu.SMEM)


def group_order(parties, lead):
    stride = max(parties // 4, 1)
    order = [m * stride + k for k in range(stride) for m in (2, 1, 3, 0) if m * stride + k < parties]
    return [lead] + [d for d in order if d != lead]


def params(limit=VMEM_BYTES):
    return pltpu.CompilerParams(vmem_limit_bytes=limit)


def local(parties, pair_rep, token_mask, ln_gain, w_proj, w_tri, gate_bias, w_out, out_bias):
    rows, length, channels = pair_rep.shape
    heads = w_tri.shape[2]
    width = w_proj.shape[2] // 4
    share = length // parties
    bias_rows = length // LANES * heads * rows
    mask = token_mask.reshape(1, length)
    w_tri = jnp.swapaxes(w_tri, 1, 2)
    shape = jax.ShapeDtypeStruct

    def full(array):
        return pl.BlockSpec(array.shape, lambda *_: (0,) * array.ndim)

    middle = parties // 2
    early = group_order(parties, (middle + 3) % parties)
    late = group_order(parties, (middle + 1) % parties)

    def ranks(order):
        return [order.index(d) for d in range(parties)]

    def exchange(parts, order):
        return lax.all_to_all(parts, "row", split_axis=0, concat_axis=0, tiled=True, axis_index_groups=[order])

    hbm = pl.BlockSpec(memory_space=pltpu.HBM)
    send = pl.pallas_call(
        bias_kernel,
        grid=(1,),
        out_shape=shape((parties, bias_rows, LANES), BF16),
        in_specs=[hbm, hbm, hbm],
        scratch_shapes=[
            pltpu.VMEM((bias_rows, LANES), F32),
            pltpu.VMEM(pair_rep.shape, F32),
            pltpu.VMEM(ln_gain.shape, F32),
            pltpu.VMEM(w_tri.shape[1:], BF16),
            pltpu.SemaphoreType.DMA((3,)),
        ],
        compiler_params=params(),
        name="bias",
    )(*(pltpu.with_memory_space_constraint(a, pltpu.HBM) for a in (pair_rep, ln_gain, w_tri)))
    got = exchange(send, early)
    kept = (w_tri, out_bias)
    q, k, v, g, column, lift = pl.pallas_call(
        functools.partial(project_kernel, heads),
        grid=(1,),
        out_shape=(
            shape((rows, width, length), BF16),
            shape((rows, length, width), BF16),
            shape((rows, width, length), BF16),
            shape((rows, width, length), F32),
            shape((length, LANES), F32),
            shape((rows, LANES), F32),
        ),
        in_specs=[full(pair_rep), full(ln_gain), SMEM, full(mask), of_pass(w_proj, 0), full(gate_bias)]
        + [full(a) for a in kept],
        compiler_params=params(),
        cost_estimate=pl.CostEstimate(
            flops=2 * rows * length * channels * 4 * width,
            transcendentals=rows * length * width,
            bytes_accessed=rows * length * width * 12,
        ),
        name="project",
    )(pair_rep, ln_gain, token_mask, mask, w_proj, gate_bias, *kept)
    taken = (pair_rep, q, k, v, g, got, column, lift, ln_gain)
    send = pl.pallas_call(
        functools.partial(first_kernel, ranks(early), ranks(late)),
        grid=(1,),
        out_shape=shape((parties, rows * share + bias_rows, LANES), BF16),
        in_specs=[full(a) for a in taken]
        + [of_pass(w_tri, 1), of_pass(w_out, 0), full(out_bias)],
        scratch_shapes=[
            pltpu.VMEM((length, heads * length), F32),
            pltpu.VMEM((bias_rows, LANES), F32),
        ],
        compiler_params=params(),
        name="first",
    )(*taken, w_tri, w_out, out_bias)
    got = exchange(send, late)
    out = pl.pallas_call(
        functools.partial(second_kernel, rows, ranks(late)),
        grid=(1,),
        out_shape=shape((length * share, channels), F32),
        in_specs=[
            full(got), full(column), full(lift), full(ln_gain), of_pass(w_proj, 1), full(gate_bias), of_pass(w_out, 1),
            full(out_bias),
        ],
        out_specs=hbm,
        scratch_shapes=[
            pltpu.VMEM((length * share, channels), F32),
            pltpu.VMEM((length, heads * length), F32),
            pltpu.SemaphoreType.DMA((length // PIECE,)),
        ],
        compiler_params=params(),
        name="second",
    )(got, column, lift, ln_gain, w_proj, gate_bias, w_out, out_bias)
    return out.reshape(length, share, channels)


def solution(mesh):
    return jax.shard_map(
        functools.partial(local, mesh.shape["row"]),
        mesh=mesh,
        in_specs=(P(("group", "row"), None, None), P("group"), P(), P(), P(), P(), P(), P()),
        out_specs=P("group", "row", None),
        check_vma=False,
    )
```

```python
import functools

import jax
import jax.numpy as jnp
from jax import lax
from jax.experimental import pallas as pl
from jax.experimental.pallas import tpu as pltpu
from jax.sharding import PartitionSpec as P

LANES = 128
VMEM_BYTES = 24 * 2**20
KEPT = 2
PIECE = 32
TOKENS = 1024
F32 = jnp.float32
BF16 = jnp.bfloat16
MASKED = -1000000000.0
EPSILON = 1e-05
LOG2E = 1.4426950408889634


def dot(a, b, dims=((1,), (0,))):
    return lax.dot_general(a, b, (dims, ((), ())), preferred_element_type=F32)


def in_step(streams, together):
    streams = list(streams)
    for at in range(0, len(streams), together):
        group = streams[at : at + together]
        while group:
            group = [stream for stream in group if next(stream, group) is not group]


def row_sums(x):
    ones = jnp.ones((x.shape[1], x.shape[1]), BF16)
    upper = x.astype(BF16)
    lower = (x - upper.astype(F32)).astype(BF16)
    return dot(upper, ones) + dot(lower, ones)


def own_rows(turned, h, heads):
    width, n = turned.shape
    dim = width // heads
    parts = [turned[h * dim : (h + 1) * dim]]
    if h:
        parts.insert(0, jnp.zeros((h * dim, n), turned.dtype))
    if h < heads - 1:
        parts.append(jnp.zeros((width - (h + 1) * dim, n), turned.dtype))
    return jnp.concatenate(parts, axis=0)


def query_block(qt, picked, heads):
    return jnp.concatenate([own_rows(qt, h, heads) for h in picked], axis=1)


def attention(k, qt, vt, gt, bias, lift, heads, result):
    dim = vt.shape[0] // heads
    weights = []
    for picked in pairs_of(heads):
        scores = dot(k, query_block(qt, picked, heads))
        for n, h in enumerate(picked):
            part = scores[:, n * LANES : (n + 1) * LANES] + bias(h)
            part = jnp.exp2(part - jnp.max(part, axis=0, keepdims=True)).astype(BF16)
            weights.append(jnp.maximum(part, lift))
            yield
    ones = jnp.ones((16, vt.shape[1]), BF16)
    mixture = []
    for picked in pairs_of(heads):
        rows = jnp.concatenate([vt[h * dim : (h + 1) * dim] for h in picked] + [ones], axis=0)
        both = dot(rows, jnp.concatenate([weights[h] for h in picked], axis=1))
        for n, h in enumerate(picked):
            column = both[:, n * LANES : (n + 1) * LANES]
            mixture.append(column[n * dim : (n + 1) * dim] * (1.0 / column[len(picked) * dim : len(picked) * dim + 1]))
        yield
    result.append((gt * jnp.concatenate(mixture, axis=0)).astype(BF16))


def turned_weights(w, width):
    sides = [w[:, at * width : (at + 1) * width] for at in (0, 2, 3)]
    return jnp.concatenate([side.T for side in sides], axis=0), w[:, width : 2 * width]


def gate_column(row, length):
    column = jnp.broadcast_to(row, (LANES, row.shape[1])).T
    return jnp.concatenate([column] * (length // LANES), axis=1)


def lift_of(row, length):
    return jnp.broadcast_to(row, (length, LANES)).astype(BF16)


def masked(part, column):
    return jnp.where(column > 0, part * LOG2E, F32(MASKED))


def projected(x, sides, keys, gate, scaling):
    width = keys.shape[1]
    three = dot(sides, x, ((1,), (1,)))
    qt = (three[:width] * scaling).astype(BF16)
    vt = three[width : 2 * width].astype(BF16)
    gt = jax.nn.sigmoid(three[2 * width :] + gate)
    return qt, dot(x, keys).astype(BF16), vt, gt


def pairs_of(heads):
    return [tuple(range(h, min(h + 2, heads))) for h in range(0, heads, 2)]


def bias_kernel(x_ref, gain_ref, w_tri_ref, send_ref, rows_ref, held_ref, scale_ref, weight_ref, sems):
    rows, length, _ = x_ref.shape
    heads = w_tri_ref.shape[1]
    copies = [
        pltpu.make_async_copy(x_ref, held_ref, sems.at[0]),
        pltpu.make_async_copy(gain_ref, scale_ref, sems.at[1]),
        pltpu.make_async_copy(w_tri_ref.at[0], weight_ref, sems.at[2]),
    ]
    for copy in copies:
        copy.start()
    for copy in copies:
        copy.wait()

    scale = scale_ref[0:1, :] * held_ref.shape[2] ** 0.5

    def stream(i, t):
        x = held_ref[i, t * LANES : (t + 1) * LANES, :]
        shifted = x - jnp.mean(x, axis=-1, keepdims=True)
        yield
        spread = row_sums(shifted * shifted)
        yield
        x = (shifted * lax.rsqrt(spread + EPSILON * x.shape[1]) * scale).astype(BF16)
        yield
        rows_ref[pl.ds(t * heads * rows + i, heads, stride=rows), :] = dot(weight_ref[...], x, ((1,), (1,)))

    in_step((stream(i, t) for i in range(rows) for t in range(length // LANES)), max(TOKENS // length, 1))
    packed = rows_ref[...].astype(BF16)
    for d in range(send_ref.shape[0]):
        send_ref[d] = packed


def project_kernel(heads, x_ref, gain_ref, flag_ref, mask_ref, w_ref, gate_bias_ref, *more_refs):
    q_ref, k_ref, v_ref, g_ref, column_ref, lift_ref = more_refs[KEPT:]
    rows, length, width = k_ref.shape
    scaling = (width // heads) ** (-0.5) * LOG2E
    sides, keys = turned_weights(w_ref[0], width)
    gate = gate_column(gate_bias_ref[0:1, :], length)
    first = lax.axis_index("row") * rows
    for i in range(rows):
        lift_ref[i : i + 1, :] = jnp.full((1, LANES), jnp.where(flag_ref[first + i] > 0, F32(0.0), F32(1.0)))
    column_ref[...] = jnp.broadcast_to((mask_ref[...] > 0).astype(F32), (LANES, length)).T
    gain = gain_ref[0:1, :] * x_ref.shape[2] ** 0.5

    def stream(i):
        x = x_ref[i]
        shifted = x - jnp.mean(x, axis=-1, keepdims=True)
        yield
        spread = row_sums(shifted * shifted)
        yield
        x = (shifted * lax.rsqrt(spread + EPSILON * x.shape[1]) * gain).astype(BF16)
        q_ref[i], k_ref[i], v_ref[i], g_ref[i] = projected(x, sides, keys, gate, scaling)

    in_step((stream(i) for i in range(rows)), max(TOKENS // length, 1))


def first_kernel(
    rank, rank_out, x_ref, q_ref, k_ref, v_ref, g_ref, got_ref, column_ref, lift_ref, gain_ref, w_tri_ref, w_out_ref,
    out_bias_ref, send_ref, bias_ref, rows_ref,
):
    rows, length, width = k_ref.shape
    heads = w_tri_ref.shape[1]
    parties = send_ref.shape[0]
    share = length // parties
    blocks = length // LANES
    reach = LANES // share
    half = heads // 2
    for h in range(heads):
        for t in range(blocks):
            at = (t * heads + h) * rows
            for b in range(blocks):
                part = jnp.concatenate(
                    [got_ref[rank[s], at : at + rows, :].astype(F32) for s in range(b * reach, (b + 1) * reach)], axis=0
                )
                span = slice(t * LANES, (t + 1) * LANES)
                bias_ref[span, (b * heads + h) * LANES : (b * heads + h + 1) * LANES] = masked(
                    part.T, column_ref[span, :]
                )
    gain = gain_ref[1:2, :] * x_ref.shape[2] ** 0.5

    def stream(i, t):
        span = slice(t * LANES, (t + 1) * LANES)
        lift = lift_of(lift_ref[i : i + 1, :], length)
        result = []

        def bias(h):
            return bias_ref[:, (t * heads + h) * LANES : (t * heads + h + 1) * LANES]

        yield from attention(
            k_ref[i], q_ref[i, :, span], v_ref[i], g_ref[i, :, span], bias, lift, heads, result
        )
        stacked = x_ref[i, span, :] + (dot(result[0], w_out_ref[0], ((0,), (0,))) + out_bias_ref[0:1, :])
        for d in range(reach):
            send_ref[rank_out[t * reach + d], i * share : (i + 1) * share, :] = stacked[
                d * share : (d + 1) * share
            ].astype(BF16)
        yield
        shifted = stacked - jnp.mean(stacked, axis=-1, keepdims=True)
        yield
        spread = row_sums(shifted * shifted)
        yield
        x = (shifted * lax.rsqrt(spread + EPSILON * stacked.shape[1]) * gain).astype(BF16)
        bias_rows = dot(w_tri_ref[0], x, ((1,), (1,)))
        for p in range(2):
            at = pl.ds((p * blocks + t) * half * rows + i, half, stride=rows)
            rows_ref[at, :] = bias_rows[p * half : (p + 1) * half]

    in_step((stream(i, t) for i in range(rows) for t in range(blocks)), max(TOKENS // length, 1))
    packed = rows_ref[...].astype(BF16)
    part = packed.shape[0] // 2
    for d in range(parties):
        send_ref[rank_out[d], rows * share :, :] = packed[d % 2 * part : (d % 2 + 1) * part]


def hold(held_ref, got_ref, rank):
    count = held_ref.shape[0] // len(rank)
    for s in range(len(rank)):
        held_ref[s * count : (s + 1) * count, :] = got_ref[rank[s], :count, :].astype(F32)


def second_project_kernel(heads, rank, got_ref, gain_ref, w_ref, gate_bias_ref, q_ref, k_ref, v_ref, g_ref, held_ref):
    share, length, width = k_ref.shape
    scaling = (width // heads) ** (-0.5) * LOG2E
    hold(held_ref, got_ref, rank)
    sides, keys = turned_weights(w_ref[0], width)
    gate = gate_column(gate_bias_ref[1:2, :], length)
    gain = gain_ref[1:2, :] * held_ref.shape[1] ** 0.5

    def stream(j):
        x = held_ref[pl.ds(j, length, stride=share), :]
        shifted = x - jnp.mean(x, axis=-1, keepdims=True)
        yield
        spread = row_sums(shifted * shifted)
        yield
        x = (shifted * lax.rsqrt(spread + EPSILON * x.shape[1]) * gain).astype(BF16)
        q_ref[j], k_ref[j], v_ref[j], g_ref[j] = projected(x, sides, keys, gate, scaling)

    in_step((stream(j) for j in range(share)), max(TOKENS // length, 1))


def second_kernel(
    rank, got_ref, other_ref, q_ref, k_ref, v_ref, g_ref, column_ref, lift_ref, w_out_ref, out_bias_ref,
    out_ref, held_ref, bias_ref, sems,
):
    parties = got_ref.shape[0]
    share, length, width = k_ref.shape
    rows = length // parties
    blocks = length // LANES
    heads = bias_ref.shape[0] // blocks
    half = heads // 2
    hold(held_ref, got_ref, rank)
    side = lax.rem(lax.axis_index("row"), 2)
    for own, ref, skip in ((side, got_ref, rows * share), (1 - side, other_ref, 0)):
        for t in range(blocks):
            for n in range(half):
                at = skip + (t * half + n) * rows
                for s in range(parties):
                    span = slice(s * rows, (s + 1) * rows)
                    bias_ref[t * heads + own * half + n, span, :] = masked(
                        ref[rank[s], at : at + rows, :].astype(F32), column_ref[span, :]
                    )

    def piece(n):
        at = pl.ds(n * PIECE * share, PIECE * share)
        return pltpu.make_async_copy(held_ref.at[at], out_ref.at[at], sems.at[n])

    copies = [piece(n) for n in range(length // PIECE)]
    stored = [0] * len(copies)
    sent = [0]

    def stream(j):
        lift = lift_of(lift_ref[j : j + 1, :], length)
        for t in range(blocks):
            span = slice(t * LANES, (t + 1) * LANES)
            result = []

            def bias(h, t=t):
                return bias_ref[t * heads + h]

            yield from attention(k_ref[j], q_ref[j, :, span], v_ref[j], g_ref[j, :, span], bias, lift, heads, result)
            update = dot(result[0], w_out_ref[0], ((0,), (0,))) + out_bias_ref[1:2, :]
            yield
            for p in range(LANES // PIECE):
                at = pl.ds((t * LANES + p * PIECE) * share + j, PIECE, stride=share)
                held_ref[at, :] = held_ref[at, :] + update[p * PIECE : (p + 1) * PIECE]
                stored[t * (LANES // PIECE) + p] += 1
                while sent[0] < len(copies) and stored[min(sent[0] + 1, len(copies) - 1)] == share:
                    copies[sent[0]].start()
                    sent[0] += 1
                yield

    in_step((stream(j) for j in range(share)), max(TOKENS // length, 1))
    for copy in copies:
        copy.wait()


def of_pass(array, p):
    shape = (1,) + array.shape[1:]
    return pl.BlockSpec(shape, lambda *_: (p,) + (0,) * (len(shape) - 1))


SMEM = pl.BlockSpec(memory_space=pltpu.SMEM)


def group_order(parties, lead):
    stride = max(parties // 4, 1)
    order = [m * stride + k for k in range(stride) for m in (2, 1, 3, 0) if m * stride + k < parties]
    return [lead] + [d for d in order if d != lead]


def params(limit=VMEM_BYTES):
    return pltpu.CompilerParams(vmem_limit_bytes=limit)


def local(parties, pair_rep, token_mask, ln_gain, w_proj, w_tri, gate_bias, w_out, out_bias):
    rows, length, channels = pair_rep.shape
    heads = w_tri.shape[2]
    width = w_proj.shape[2] // 4
    share = length // parties
    bias_rows = length // LANES * heads * rows
    mask = token_mask.reshape(1, length)
    w_tri = jnp.swapaxes(w_tri, 1, 2)
    shape = jax.ShapeDtypeStruct

    def full(array):
        return pl.BlockSpec(array.shape, lambda *_: (0,) * array.ndim)

    middle = parties // 2
    early = group_order(parties, (middle + 3) % parties)
    late = group_order(parties, (middle + 1) % parties)

    def ranks(order):
        return [order.index(d) for d in range(parties)]

    def exchange(parts, order):
        return lax.all_to_all(parts, "row", split_axis=0, concat_axis=0, tiled=True, axis_index_groups=[order])

    hbm = pl.BlockSpec(memory_space=pltpu.HBM)
    send = pl.pallas_call(
        bias_kernel,
        grid=(1,),
        out_shape=shape((parties, bias_rows, LANES), BF16),
        in_specs=[hbm, hbm, hbm],
        scratch_shapes=[
            pltpu.VMEM((bias_rows, LANES), F32),
            pltpu.VMEM(pair_rep.shape, F32),
            pltpu.VMEM(ln_gain.shape, F32),
            pltpu.VMEM(w_tri.shape[1:], BF16),
            pltpu.SemaphoreType.DMA((3,)),
        ],
        compiler_params=params(),
        name="bias",
    )(*(pltpu.with_memory_space_constraint(a, pltpu.HBM) for a in (pair_rep, ln_gain, w_tri)))
    got = exchange(send, early)
    kept = (w_tri, out_bias)
    q, k, v, g, column, lift = pl.pallas_call(
        functools.partial(project_kernel, heads),
        grid=(1,),
        out_shape=(
            shape((rows, width, length), BF16),
            shape((rows, length, width), BF16),
            shape((rows, width, length), BF16),
            shape((rows, width, length), F32),
            shape((length, LANES), F32),
            shape((rows, LANES), F32),
        ),
        in_specs=[full(pair_rep), full(ln_gain), SMEM, full(mask), of_pass(w_proj, 0), full(gate_bias)]
        + [full(a) for a in kept],
        compiler_params=params(),
        cost_estimate=pl.CostEstimate(
            flops=2 * rows * length * channels * 4 * width,
            transcendentals=rows * length * width,
            bytes_accessed=rows * length * width * 12,
        ),
        name="project",
    )(pair_rep, ln_gain, token_mask, mask, w_proj, gate_bias, *kept)
    taken = (pair_rep, q, k, v, g, got, column, lift, ln_gain)
    send = pl.pallas_call(
        functools.partial(first_kernel, ranks(early), ranks(late)),
        grid=(1,),
        out_shape=shape((parties, rows * share + bias_rows // 2, LANES), BF16),
        in_specs=[full(a) for a in taken]
        + [of_pass(w_tri, 1), of_pass(w_out, 0), full(out_bias)],
        scratch_shapes=[
            pltpu.VMEM((length, heads * length), F32),
            pltpu.VMEM((bias_rows, LANES), F32),
        ],
        compiler_params=params(),
        name="first",
    )(*taken, w_tri, w_out, out_bias)
    got = exchange(send, late)
    partners = [(d, d ^ 1) for d in range(parties)]
    other = lax.ppermute(got[:, rows * share :, :], "row", partners)
    q, k, v, g = pl.pallas_call(
        functools.partial(second_project_kernel, heads, ranks(late)),
        grid=(1,),
        out_shape=(
            shape((share, width, length), BF16),
            shape((share, length, width), BF16),
            shape((share, width, length), BF16),
            shape((share, width, length), F32),
        ),
        in_specs=[full(got), full(ln_gain), of_pass(w_proj, 1), full(gate_bias)],
        scratch_shapes=[pltpu.VMEM((length * share, channels), F32)],
        compiler_params=params(),
        cost_estimate=pl.CostEstimate(
            flops=2 * rows * length * channels * 4 * width,
            transcendentals=rows * length * width,
            bytes_accessed=rows * length * width * 12,
        ),
        name="second_project",
    )(got, ln_gain, w_proj, gate_bias)
    taken = (got, other, q, k, v, g, column, lift)
    out = pl.pallas_call(
        functools.partial(second_kernel, ranks(late)),
        grid=(1,),
        out_shape=shape((length * share, channels), F32),
        in_specs=[full(a) for a in taken] + [of_pass(w_out, 1), full(out_bias)],
        out_specs=hbm,
        scratch_shapes=[
            pltpu.VMEM((length * share, channels), F32),
            pltpu.VMEM((length // LANES * heads, length, LANES), F32),
            pltpu.SemaphoreType.DMA((length // PIECE,)),
        ],
        compiler_params=params(),
        name="second",
    )(*taken, w_out, out_bias)
    return out.reshape(length, share, channels)


def solution(mesh):
    return jax.shard_map(
        functools.partial(local, mesh.shape["row"]),
        mesh=mesh,
        in_specs=(P(("group", "row"), None, None), P("group"), P(), P(), P(), P(), P(), P()),
        out_specs=P("group", "row", None),
        check_vma=False,
    )
```

```python
import functools

import jax
import jax.numpy as jnp
from jax import lax
from jax.experimental import pallas as pl
from jax.experimental.pallas import tpu as pltpu
from jax.sharding import PartitionSpec as P

LANES = 128
VMEM_BYTES = 24 * 2**20
KEPT = 2
PIECE = 64
TOKENS = 1024
F32 = jnp.float32
BF16 = jnp.bfloat16
MASKED = -1000000000.0
EPSILON = 1e-05
LOG2E = 1.4426950408889634


def dot(a, b, dims=((1,), (0,))):
    return lax.dot_general(a, b, (dims, ((), ())), preferred_element_type=F32)


def in_step(streams, together):
    streams = list(streams)
    for at in range(0, len(streams), together):
        group = streams[at : at + together]
        while group:
            group = [stream for stream in group if next(stream, group) is not group]


def row_sums(x):
    ones = jnp.ones((x.shape[1], x.shape[1]), BF16)
    upper = x.astype(BF16)
    lower = (x - upper.astype(F32)).astype(BF16)
    return dot(upper, ones) + dot(lower, ones)


def own_rows(turned, h, heads):
    width, n = turned.shape
    dim = width // heads
    parts = [turned[h * dim : (h + 1) * dim]]
    if h:
        parts.insert(0, jnp.zeros((h * dim, n), turned.dtype))
    if h < heads - 1:
        parts.append(jnp.zeros((width - (h + 1) * dim, n), turned.dtype))
    return jnp.concatenate(parts, axis=0)


def query_block(qt, picked, heads):
    return jnp.concatenate([own_rows(qt, h, heads) for h in picked], axis=1)


def attention(k, qt, vt, gt, bias, lift, heads, result):
    dim = vt.shape[0] // heads
    weights = []
    for picked in pairs_of(heads):
        scores = dot(k, query_block(qt, picked, heads))
        for n, h in enumerate(picked):
            part = scores[:, n * LANES : (n + 1) * LANES] + bias(h)
            part = jnp.exp2(part - jnp.max(part, axis=0, keepdims=True)).astype(BF16)
            weights.append(jnp.maximum(part, lift))
            yield
    ones = jnp.ones((16, vt.shape[1]), BF16)
    mixture = []
    for picked in pairs_of(heads):
        rows = jnp.concatenate([vt[h * dim : (h + 1) * dim] for h in picked] + [ones], axis=0)
        both = dot(rows, jnp.concatenate([weights[h] for h in picked], axis=1))
        for n, h in enumerate(picked):
            column = both[:, n * LANES : (n + 1) * LANES]
            mixture.append(column[n * dim : (n + 1) * dim] * (1.0 / column[len(picked) * dim : len(picked) * dim + 1]))
        yield
    result.append((gt * jnp.concatenate(mixture, axis=0)).astype(BF16))


def turned_weights(w, width):
    sides = [w[:, at * width : (at + 1) * width] for at in (0, 2, 3)]
    return jnp.concatenate([side.T for side in sides], axis=0), w[:, width : 2 * width]


def gate_column(row, length):
    column = jnp.broadcast_to(row, (LANES, row.shape[1])).T
    return jnp.concatenate([column] * (length // LANES), axis=1)


def lift_of(row, length):
    return jnp.broadcast_to(row, (length, LANES)).astype(BF16)


def masked(part, column):
    return jnp.where(column > 0, part * LOG2E, F32(MASKED))


def projected(x, sides, keys, gate, scaling):
    width = keys.shape[1]
    three = dot(sides, x, ((1,), (1,)))
    qt = (three[:width] * scaling).astype(BF16)
    vt = three[width : 2 * width].astype(BF16)
    gt = jax.nn.sigmoid(three[2 * width :] + gate)
    return qt, dot(x, keys).astype(BF16), vt, gt


def pairs_of(heads):
    return [tuple(range(h, min(h + 2, heads))) for h in range(0, heads, 2)]


def bias_kernel(x_ref, gain_ref, w_tri_ref, send_ref, rows_ref, held_ref, scale_ref, weight_ref, sems):
    rows, length, _ = x_ref.shape
    heads = w_tri_ref.shape[1]
    copies = [
        pltpu.make_async_copy(x_ref, held_ref, sems.at[0]),
        pltpu.make_async_copy(gain_ref, scale_ref, sems.at[1]),
        pltpu.make_async_copy(w_tri_ref.at[0], weight_ref, sems.at[2]),
    ]
    for copy in copies:
        copy.start()
    for copy in copies:
        copy.wait()

    scale = scale_ref[0:1, :] * held_ref.shape[2] ** 0.5

    def stream(i, t):
        x = held_ref[i, t * LANES : (t + 1) * LANES, :]
        shifted = x - jnp.mean(x, axis=-1, keepdims=True)
        yield
        spread = row_sums(shifted * shifted)
        yield
        x = (shifted * lax.rsqrt(spread + EPSILON * x.shape[1]) * scale).astype(BF16)
        yield
        rows_ref[pl.ds(t * heads * rows + i, heads, stride=rows), :] = dot(weight_ref[...], x, ((1,), (1,)))

    in_step((stream(i, t) for i in range(rows) for t in range(length // LANES)), max(TOKENS // length, 1))
    packed = rows_ref[...].astype(BF16)
    for d in range(send_ref.shape[0]):
        send_ref[d] = packed


def project_kernel(heads, x_ref, gain_ref, flag_ref, mask_ref, w_ref, gate_bias_ref, *more_refs):
    q_ref, k_ref, v_ref, g_ref, column_ref, lift_ref = more_refs[KEPT:]
    rows, length, width = k_ref.shape
    scaling = (width // heads) ** (-0.5) * LOG2E
    sides, keys = turned_weights(w_ref[0], width)
    gate = gate_column(gate_bias_ref[0:1, :], length)
    first = lax.axis_index("row") * rows
    for i in range(rows):
        lift_ref[i : i + 1, :] = jnp.full((1, LANES), jnp.where(flag_ref[first + i] > 0, F32(0.0), F32(1.0)))
    column_ref[...] = jnp.broadcast_to((mask_ref[...] > 0).astype(F32), (LANES, length)).T
    gain = gain_ref[0:1, :] * x_ref.shape[2] ** 0.5

    def stream(i):
        x = x_ref[i]
        shifted = x - jnp.mean(x, axis=-1, keepdims=True)
        yield
        spread = row_sums(shifted * shifted)
        yield
        x = (shifted * lax.rsqrt(spread + EPSILON * x.shape[1]) * gain).astype(BF16)
        q_ref[i], k_ref[i], v_ref[i], g_ref[i] = projected(x, sides, keys, gate, scaling)

    in_step((stream(i) for i in range(rows)), max(TOKENS // length, 1))


def first_kernel(
    rank, rank_out, x_ref, q_ref, k_ref, v_ref, g_ref, got_ref, column_ref, lift_ref, gain_ref, w_tri_ref, w_out_ref,
    out_bias_ref, send_ref, bias_ref, rows_ref,
):
    rows, length, width = k_ref.shape
    heads = w_tri_ref.shape[1]
    parties = send_ref.shape[0]
    share = length // parties
    blocks = length // LANES
    reach = LANES // share
    half = heads // 2
    for h in range(heads):
        for t in range(blocks):
            at = (t * heads + h) * rows
            for b in range(blocks):
                part = jnp.concatenate(
                    [got_ref[rank[s], at : at + rows, :].astype(F32) for s in range(b * reach, (b + 1) * reach)], axis=0
                )
                span = slice(t * LANES, (t + 1) * LANES)
                bias_ref[span, (b * heads + h) * LANES : (b * heads + h + 1) * LANES] = masked(
                    part.T, column_ref[span, :]
                )
    gain = gain_ref[1:2, :] * x_ref.shape[2] ** 0.5

    def stream(i, t):
        span = slice(t * LANES, (t + 1) * LANES)
        lift = lift_of(lift_ref[i : i + 1, :], length)
        result = []

        def bias(h):
            return bias_ref[:, (t * heads + h) * LANES : (t * heads + h + 1) * LANES]

        yield from attention(
            k_ref[i], q_ref[i, :, span], v_ref[i], g_ref[i, :, span], bias, lift, heads, result
        )
        stacked = x_ref[i, span, :] + (dot(result[0], w_out_ref[0], ((0,), (0,))) + out_bias_ref[0:1, :])
        for d in range(reach):
            send_ref[rank_out[t * reach + d], i * share : (i + 1) * share, :] = stacked[
                d * share : (d + 1) * share
            ].astype(BF16)
        yield
        shifted = stacked - jnp.mean(stacked, axis=-1, keepdims=True)
        yield
        spread = row_sums(shifted * shifted)
        yield
        x = (shifted * lax.rsqrt(spread + EPSILON * stacked.shape[1]) * gain).astype(BF16)
        bias_rows = dot(w_tri_ref[0], x, ((1,), (1,)))
        for p in range(2):
            at = pl.ds((p * blocks + t) * half * rows + i, half, stride=rows)
            rows_ref[at, :] = bias_rows[p * half : (p + 1) * half]

    in_step((stream(i, t) for i in range(rows) for t in range(blocks)), max(TOKENS // length, 1))
    packed = rows_ref[...].astype(BF16)
    part = packed.shape[0] // 2
    for d in range(parties):
        send_ref[rank_out[d], rows * share :, :] = packed[d % 2 * part : (d % 2 + 1) * part]


def hold(held_ref, got_ref, rank):
    count = held_ref.shape[0] // len(rank)
    for s in range(len(rank)):
        held_ref[s * count : (s + 1) * count, :] = got_ref[rank[s], :count, :].astype(F32)


def second_project_kernel(heads, rank, got_ref, gain_ref, w_ref, gate_bias_ref, q_ref, k_ref, v_ref, g_ref, held_ref):
    share, length, width = k_ref.shape
    scaling = (width // heads) ** (-0.5) * LOG2E
    hold(held_ref, got_ref, rank)
    sides, keys = turned_weights(w_ref[0], width)
    gate = gate_column(gate_bias_ref[1:2, :], length)
    gain = gain_ref[1:2, :] * held_ref.shape[1] ** 0.5

    def stream(j):
        x = held_ref[pl.ds(j, length, stride=share), :]
        shifted = x - jnp.mean(x, axis=-1, keepdims=True)
        yield
        spread = row_sums(shifted * shifted)
        yield
        x = (shifted * lax.rsqrt(spread + EPSILON * x.shape[1]) * gain).astype(BF16)
        q_ref[j], k_ref[j], v_ref[j], g_ref[j] = projected(x, sides, keys, gate, scaling)

    in_step((stream(j) for j in range(share)), max(TOKENS // length, 1))


def second_kernel(
    rank, got_ref, other_ref, stacked_ref, q_ref, k_ref, v_ref, g_ref, column_ref, lift_ref, w_out_ref, out_bias_ref,
    out_ref, held_ref, bias_ref, sems,
):
    parties = got_ref.shape[0]
    share, length, width = k_ref.shape
    rows = length // parties
    blocks = length // LANES
    heads = bias_ref.shape[0] // blocks
    half = heads // 2
    side = lax.rem(lax.axis_index("row"), 2)
    for own, ref, skip in ((side, got_ref, rows * share), (1 - side, other_ref, 0)):
        for t in range(blocks):
            for n in range(half):
                at = skip + (t * half + n) * rows
                for s in range(parties):
                    span = slice(s * rows, (s + 1) * rows)
                    bias_ref[t * heads + own * half + n, span, :] = masked(
                        ref[rank[s], at : at + rows, :].astype(F32), column_ref[span, :]
                    )

    def piece(n):
        at = pl.ds(n * PIECE * share, PIECE * share)
        return pltpu.make_async_copy(held_ref.at[at], out_ref.at[at], sems.at[n])

    copies = [piece(n) for n in range(length // PIECE)]
    stored = [0] * len(copies)
    sent = [0]

    def stream(j):
        lift = lift_of(lift_ref[j : j + 1, :], length)
        for t in range(blocks):
            span = slice(t * LANES, (t + 1) * LANES)
            result = []

            def bias(h, t=t):
                return bias_ref[t * heads + h]

            yield from attention(k_ref[j], q_ref[j, :, span], v_ref[j], g_ref[j, :, span], bias, lift, heads, result)
            update = dot(result[0], w_out_ref[0], ((0,), (0,))) + out_bias_ref[1:2, :]
            yield
            for p in range(LANES // PIECE):
                at = pl.ds((t * LANES + p * PIECE) * share + j, PIECE, stride=share)
                held_ref[at, :] = stacked_ref[at, :] + update[p * PIECE : (p + 1) * PIECE]
                stored[t * (LANES // PIECE) + p] += 1
                while sent[0] < len(copies) and stored[min(sent[0] + 1, len(copies) - 1)] == share:
                    copies[sent[0]].start()
                    sent[0] += 1
                yield

    in_step((stream(j) for j in range(share)), max(TOKENS // length, 1))
    for copy in copies:
        copy.wait()


def of_pass(array, p):
    shape = (1,) + array.shape[1:]
    return pl.BlockSpec(shape, lambda *_: (p,) + (0,) * (len(shape) - 1))


SMEM = pl.BlockSpec(memory_space=pltpu.SMEM)


def group_order(parties, lead):
    stride = max(parties // 4, 1)
    order = [m * stride + k for k in range(stride) for m in (2, 1, 3, 0) if m * stride + k < parties]
    return [lead] + [d for d in order if d != lead]


def params(limit=VMEM_BYTES):
    return pltpu.CompilerParams(vmem_limit_bytes=limit)


def local(parties, pair_rep, token_mask, ln_gain, w_proj, w_tri, gate_bias, w_out, out_bias):
    rows, length, channels = pair_rep.shape
    heads = w_tri.shape[2]
    width = w_proj.shape[2] // 4
    share = length // parties
    bias_rows = length // LANES * heads * rows
    mask = token_mask.reshape(1, length)
    w_tri = jnp.swapaxes(w_tri, 1, 2)
    shape = jax.ShapeDtypeStruct

    def full(array):
        return pl.BlockSpec(array.shape, lambda *_: (0,) * array.ndim)

    middle = parties // 2
    early = group_order(parties, (middle + 3) % parties)
    late = group_order(parties, (middle + 1) % parties)

    def ranks(order):
        return [order.index(d) for d in range(parties)]

    def exchange(parts, order):
        return lax.all_to_all(parts, "row", split_axis=0, concat_axis=0, tiled=True, axis_index_groups=[order])

    hbm = pl.BlockSpec(memory_space=pltpu.HBM)
    send = pl.pallas_call(
        bias_kernel,
        grid=(1,),
        out_shape=shape((parties, bias_rows, LANES), BF16),
        in_specs=[hbm, hbm, hbm],
        scratch_shapes=[
            pltpu.VMEM((bias_rows, LANES), F32),
            pltpu.VMEM(pair_rep.shape, F32),
            pltpu.VMEM(ln_gain.shape, F32),
            pltpu.VMEM(w_tri.shape[1:], BF16),
            pltpu.SemaphoreType.DMA((3,)),
        ],
        compiler_params=params(),
        name="bias",
    )(*(pltpu.with_memory_space_constraint(a, pltpu.HBM) for a in (pair_rep, ln_gain, w_tri)))
    got = exchange(send, early)
    kept = (w_tri, out_bias)
    q, k, v, g, column, lift = pl.pallas_call(
        functools.partial(project_kernel, heads),
        grid=(1,),
        out_shape=(
            shape((rows, width, length), BF16),
            shape((rows, length, width), BF16),
            shape((rows, width, length), BF16),
            shape((rows, width, length), F32),
            shape((length, LANES), F32),
            shape((rows, LANES), F32),
        ),
        in_specs=[full(pair_rep), full(ln_gain), SMEM, full(mask), of_pass(w_proj, 0), full(gate_bias)]
        + [full(a) for a in kept],
        compiler_params=params(),
        cost_estimate=pl.CostEstimate(
            flops=2 * rows * length * channels * 4 * width,
            transcendentals=rows * length * width,
            bytes_accessed=rows * length * width * 12,
        ),
        name="project",
    )(pair_rep, ln_gain, token_mask, mask, w_proj, gate_bias, *kept)
    taken = (pair_rep, q, k, v, g, got, column, lift, ln_gain)
    send = pl.pallas_call(
        functools.partial(first_kernel, ranks(early), ranks(late)),
        grid=(1,),
        out_shape=shape((parties, rows * share + bias_rows // 2, LANES), BF16),
        in_specs=[full(a) for a in taken]
        + [of_pass(w_tri, 1), of_pass(w_out, 0), full(out_bias)],
        scratch_shapes=[
            pltpu.VMEM((length, heads * length), F32),
            pltpu.VMEM((bias_rows, LANES), F32),
        ],
        compiler_params=params(),
        name="first",
    )(*taken, w_tri, w_out, out_bias)
    got = exchange(send, late)
    partners = [(d, d ^ 1) for d in range(parties)]
    other = lax.ppermute(got[:, rows * share :, :], "row", partners)
    q, k, v, g, stacked = pl.pallas_call(
        functools.partial(second_project_kernel, heads, ranks(late)),
        grid=(1,),
        out_shape=(
            shape((share, width, length), BF16),
            shape((share, length, width), BF16),
            shape((share, width, length), BF16),
            shape((share, width, length), F32),
            shape((length * share, channels), F32),
        ),
        in_specs=[full(got), full(ln_gain), of_pass(w_proj, 1), full(gate_bias)],
        compiler_params=params(),
        cost_estimate=pl.CostEstimate(
            flops=2 * rows * length * channels * 4 * width,
            transcendentals=rows * length * width,
            bytes_accessed=rows * length * width * 12,
        ),
        name="second_project",
    )(got, ln_gain, w_proj, gate_bias)
    taken = (got, other, stacked, q, k, v, g, column, lift)
    out = pl.pallas_call(
        functools.partial(second_kernel, ranks(late)),
        grid=(1,),
        out_shape=shape((length * share, channels), F32),
        in_specs=[full(a) for a in taken] + [of_pass(w_out, 1), full(out_bias)],
        out_specs=hbm,
        scratch_shapes=[
            pltpu.VMEM((length * share, channels), F32),
            pltpu.VMEM((length // LANES * heads, length, LANES), F32),
            pltpu.SemaphoreType.DMA((length // PIECE,)),
        ],
        compiler_params=params(),
        name="second",
    )(*taken, w_out, out_bias)
    return out.reshape(length, share, channels)


def solution(mesh):
    return jax.shard_map(
        functools.partial(local, mesh.shape["row"]),
        mesh=mesh,
        in_specs=(P(("group", "row"), None, None), P("group"), P(), P(), P(), P(), P(), P()),
        out_specs=P("group", "row", None),
        check_vma=False,
    )
```
